768 devices in a mesh: heads: 4 (over x), team: 2 (over core), blk: 96 (over z, y).
Axes of the slice: x: 4, y: 8, z: 12, core: 2. Of those that a mesh axis runs over, the one named last changes fastest.
Arguments:
- queries: bfloat16 [4, 3072, 32, 128], P('heads', ('team', 'blk')), may hold values from -26 to 26
- keys: bfloat16 [4, 3072, 8, 128], P('heads', ('team', 'blk')), may hold values from -26 to 26
- values: bfloat16 [4, 3072, 8, 128], P('heads', ('team', 'blk')), may hold values from -6 to 6
- run_index: int32 [192], replicated, may hold values from 0 to 191, each once
Outputs:
- attended: bfloat16 [12288, 32, 128], P(('team', 'blk'), 'heads')
The draws below stay inside these ranges and needn't reach their ends.
All inputs are finite; a program needn't handle non-finite values.
Results may differ from the reference program's by a relative error of at most 0.012.
The reference program's roundings to bfloat16 on the way count: a program that leaves them out, or rounds other values in their place, can miss the bound.
Values may be sent and summed in bfloat16 or wider, within the bound.
No kernel may reach another device: no remote copies, remote signals or barrier semaphores. Data moves between devices by JAX's collectives and lax.ppermute only.
A program may use at most 32 MiB of HBM per device.

```python
import math
import jax
import jax.numpy as jnp
from jax import lax

HD = 128
QH = 32
KVH = 8
ROW_DEV = 64
SPLITS = 4
PIECE = 16
SLOTS = 192
SEQ = 12288


def draw_queries(key, part):
    shape = (SPLITS, SLOTS * PIECE, QH, HD)
    base = 1.7 * jax.random.normal(jax.random.fold_in(key, 11), shape, jnp.float32)
    return jnp.clip(base, -26.0, 26.0).astype(jnp.bfloat16)


def draw_keys(key, part):
    shape = (SPLITS, SLOTS * PIECE, KVH, HD)
    base = 1.7 * jax.random.normal(jax.random.fold_in(key, 21), shape, jnp.float32)
    return jnp.clip(base, -26.0, 26.0).astype(jnp.bfloat16)


def steps_of(own_key, shape, pieces, smallest, top_value):
    loudness, own = 1.0, jax.random.fold_in(own_key, 6)
    for axis_at, shards_of in pieces:
        heights = jnp.exp(jax.random.uniform(jax.random.fold_in(own, axis_at), (shards_of,), jnp.float32, smallest / len(pieces), top_value / len(pieces)))
        loudness = loudness * jnp.repeat(heights, shape[axis_at] // shards_of).reshape([-1 if axis == axis_at else 1 for axis in range(len(shape))])
    return loudness


def normal_values(own_key, dims, deviation, limit, cuts=(), kind=jnp.bfloat16):
    drawn = deviation * jax.random.normal(own_key, dims, jnp.float32)
    if cuts:
        drawn = drawn * steps_of(own_key, dims, cuts, -0.22, 0.18)
    return jnp.clip(drawn, -limit, limit).astype(kind)


def setup_inputs(seed: int = 0) -> dict:
    key_of = jax.random.split(jax.random.key(seed), 5)
    return {
        "queries": draw_queries(jax.random.fold_in(key_of[4], 71), 0),
        "keys": draw_keys(jax.random.fold_in(key_of[4], 71), 0),
        "values": normal_values(key_of[2], (SPLITS, SLOTS * PIECE, KVH, HD), 1.0, 6.0, ((0, 4), (1, 192))),
        "run_index": jax.random.permutation(key_of[3], SLOTS).astype(jnp.int32),
    }


rope_theta = 500000.0
rope_factor = 8.0
low_factor = 1.0
high_factor = 4.0
initial_context = 8192.0


def inverse_freqs(head_width):
    half_width = head_width // 2
    counter = jnp.arange(half_width, dtype=jnp.float32)
    base_freq = 1.0 / (rope_theta ** (2.0 * counter / head_width))
    wavelength = 2.0 * jnp.pi / base_freq
    smooth = (initial_context / wavelength - low_factor) / (high_factor - low_factor)
    blended = (1.0 - smooth) * base_freq / rope_factor + smooth * base_freq
    middle = jnp.where(wavelength > initial_context / low_factor, base_freq / rope_factor, blended)
    return jnp.where(wavelength < initial_context / high_factor, base_freq, middle)


def rotate_heads(values_in, positions, inverse):
    half_width = values_in.shape[-1] // 2
    angles = positions.astype(jnp.float32)[:, None] * inverse[None, :]
    cosine = jnp.cos(angles)[:, None, :]
    sine_part = jnp.sin(angles)[:, None, :]
    first_half = values_in[..., :half_width]
    second = values_in[..., half_width:]
    return jnp.concatenate([first_half * cosine - second * sine_part, second * cosine + first_half * sine_part], axis=-1)


def slot_order(array):
    heads_here = array.shape[2]
    grid = array.reshape(SPLITS, SLOTS, PIECE, heads_here, HD)
    return jnp.transpose(grid, (1, 0, 2, 3, 4)).reshape(SEQ, heads_here, HD)


def reference(queries, keys, values, run_index):
    all_rows = jnp.arange(SEQ, dtype=jnp.int32)
    slot_ids = all_rows // ROW_DEV
    local_rows = all_rows % ROW_DEV
    run_ids = run_index[slot_ids].astype(jnp.int32)
    half_rows = ROW_DEV // 2
    early_at = run_ids * half_rows + local_rows
    late_at = (2 * SLOTS - 1 - run_ids) * half_rows + local_rows - half_rows
    positions = jnp.where(local_rows < half_rows, early_at, late_at).astype(jnp.int32)
    inverse = inverse_freqs(HD)
    rot_q = rotate_heads(slot_order(queries).astype(jnp.float32), positions, inverse).astype(jnp.bfloat16)
    rot_k = rotate_heads(slot_order(keys).astype(jnp.float32), positions, inverse).astype(jnp.bfloat16)
    ordered_v = slot_order(values)
    group_size = QH // KVH
    scaling = HD ** -0.5
    block_rows = ROW_DEV * math.gcd(SLOTS, max(1, 768 // ROW_DEV))
    block_count = SEQ // block_rows
    grouped_q = rot_q.reshape(block_count, block_rows, KVH, group_size, HD)
    pos_blocks = positions.reshape(block_count, block_rows)

    def attend_block(packed):
        query_block, query_pos = packed
        visible = (positions[None, :] <= query_pos[:, None])[None]

        def per_head(head_id):
            head_q = lax.dynamic_index_in_dim(query_block, head_id, 1, keepdims=False).astype(jnp.float32)
            head_k = lax.dynamic_index_in_dim(rot_k, head_id, 1, keepdims=False).astype(jnp.float32)
            head_v = lax.dynamic_index_in_dim(ordered_v, head_id, 1, keepdims=False).astype(jnp.float32)
            scores = jnp.einsum("bgd,kd->gbk", head_q, head_k) * scaling
            scores = jnp.where(visible, scores, -jnp.inf)
            highest = jnp.max(scores, axis=-1, keepdims=True)
            weights = jnp.exp(scores - highest)
            denominator = jnp.sum(weights, axis=-1)
            rounded = lax.optimization_barrier(weights.astype(jnp.bfloat16)).astype(jnp.float32)
            mixed = jnp.einsum("gbk,kd->gbd", rounded, head_v)
            return mixed / denominator[..., None]

        per_group = lax.map(per_head, jnp.arange(KVH, dtype=jnp.int32))
        return jnp.transpose(per_group, (2, 0, 1, 3)).reshape(block_rows, QH, HD)

    attended = lax.map(attend_block, (grouped_q, pos_blocks))
    return attended.reshape(SEQ, QH, HD).astype(jnp.bfloat16)
```

```python
import math

import jax
import jax.numpy as jnp
from jax import lax
from jax.experimental import pallas as pl
from jax.experimental.pallas import tpu as pltpu
from jax.sharding import Mesh, PartitionSpec as P

mask_floor = -1e30
rope_theta = 500000.0
rope_factor = 8.0
low_factor = 1.0
high_factor = 4.0
initial_context = 8192.0

X, T, Z, Y = 4, 2, 12, 8
PIECE = 16
HALF = 32
GROUP = 4
HD = 128
SLOTS = T * Z * Y
Q_ROWS = GROUP * PIECE
KEYS = Z * T * 2 * PIECE
LANES = 2 * Q_ROWS
MSG = 2 * HD + 16
LOG2_SCALE = HD ** -0.5 * math.log2(math.e)


def inverse_freqs(head_width):
    half_width = head_width // 2
    counter = jnp.arange(half_width, dtype=jnp.float32)
    base_freq = 1.0 / rope_theta ** (2.0 * counter / head_width)
    wavelength = 2.0 * jnp.pi / base_freq
    smooth = (initial_context / wavelength - low_factor) / (high_factor - low_factor)
    blended = (1.0 - smooth) * base_freq / rope_factor + smooth * base_freq
    middle = jnp.where(wavelength > initial_context / low_factor, base_freq / rope_factor, blended)
    return jnp.where(wavelength < initial_context / high_factor, base_freq, middle)


def rotate(x, cosine, sine):
    half = HD // 2
    first, second = x[..., :half], x[..., half:]
    return jnp.concatenate(
        [first * cosine - second * sine, second * cosine + first * sine], axis=-1
    ).astype(jnp.bfloat16)


def attend_kernel(q_run, k_run, q_ref, kv_ref, o_ref, k_s, vt_s, kpos_s):
    bf, f32 = jnp.bfloat16, jnp.float32
    for half in range(2):
        picked = kv_ref[:, 2 * half : 2 * half + 2]
        rows = slice(half * KEYS, (half + 1) * KEYS)
        k_s[rows, :] = picked[:, :, :, 0].reshape(KEYS, HD)
        vt_s[:, rows] = picked[:, :, :, 1].reshape(KEYS, HD).T
    row = lax.broadcasted_iota(jnp.int32, (PIECE, HD), 0)
    for z in range(Z):
        for x in range(4):
            for t in range(T):
                run = k_run[t * Z + z]
                base = run * HALF if x < 2 else (2 * SLOTS - 1 - run) * HALF
                at = (x // 2) * KEYS + ((z * 2 + x % 2) * T + t) * PIECE
                kpos_s[at : at + PIECE, :] = row + (base + (x % 2) * PIECE)
    lane = lax.broadcasted_iota(jnp.int32, (1, LANES), 1)
    local = (lane // Q_ROWS) * PIECE + lane % PIECE

    def softmax_part(q_tile, q_pos, n_keys, n_free):
        s = lax.dot_general(
            k_s[:n_keys, :], q_tile, (((1,), (1,)), ((), ())), preferred_element_type=f32
        )
        kp = kpos_s[n_free:n_keys, :]
        visible = jnp.concatenate([kp, kp], axis=1) <= q_pos
        tail = jnp.where(visible, s[n_free:], mask_floor)
        s = jnp.concatenate([s[:n_free], tail], axis=0) if n_free else tail
        top = jnp.max(s, axis=0, keepdims=True)
        w = jnp.exp2((s - top) * LOG2_SCALE)
        total = jnp.sum(w, axis=0, keepdims=True)
        o = lax.dot_general(
            vt_s[:, :n_keys], w.astype(bf), (((1,), (0,)), ((), ())), preferred_element_type=f32
        )
        lse = top * LOG2_SCALE + jnp.log2(total)
        hi = lse.astype(bf).astype(f32)
        mid = (lse - hi).astype(bf).astype(f32)
        low = lse - hi - mid
        return (o * (1.0 / total)).astype(bf), [hi, mid, low]

    def step(y, carry):
        def tile(x0):
            return jnp.concatenate(
                [q_ref[y, x0 + x, t] for t in range(T) for x in range(2)], axis=0
            )

        runs = [q_run[t * Y + y] for t in range(T)]
        pos_e = jnp.concatenate([local + r * HALF for r in runs], axis=1)
        pos_l = jnp.concatenate([local + (2 * SLOTS - 1 - r) * HALF for r in runs], axis=1)
        o_e, st_e = softmax_part(tile(0), pos_e, KEYS, 0)
        o_l, st_l = softmax_part(tile(2), pos_l, 2 * KEYS, KEYS)
        pad = jnp.zeros((10, LANES), f32)
        for t in range(T):
            cols = slice(t * LANES, (t + 1) * LANES)
            o_ref[t, y, :HD, :] = o_e[:, cols]
            o_ref[t, y, HD : 2 * HD, :] = o_l[:, cols]
            stats = jnp.concatenate([v[:, cols] for v in st_e + st_l] + [pad], axis=0)
            o_ref[t, y, 2 * HD :, :] = stats.astype(bf)
        return carry

    lax.fori_loop(0, Y, step, 0)


def combine_kernel(r_ref, o_ref):
    f32 = jnp.float32
    for half in range(2):
        heads = []
        for t in range(T):
            lse = []
            for y in range(Y):
                st = r_ref[t, y, 2 * HD :, :].astype(f32)
                at = 3 * half
                lse.append(st[at : at + 1] + st[at + 1 : at + 2] + st[at + 2 : at + 3])
            top = lse[0]
            for v in lse[1:]:
                top = jnp.maximum(top, v)
            ws = [jnp.exp2(v - top) for v in lse]
            total = ws[0]
            for v in ws[1:]:
                total = total + v
            acc = jnp.zeros((HD, LANES), f32)
            for y in range(Y):
                acc = acc + r_ref[t, y, half * HD : (half + 1) * HD, :].astype(f32) * ws[y]
            heads.append((acc * (1.0 / total)).T)
        for p in range(2):
            for t in range(T):
                for j in range(GROUP):
                    at = p * Q_ROWS + j * PIECE
                    rows = slice(half * HALF + p * PIECE, half * HALF + (p + 1) * PIECE)
                    o_ref[t * GROUP + j, rows, :] = heads[t][at : at + PIECE].astype(jnp.bfloat16)


def per_device(queries, keys, values, run_index):
    bf, f32 = jnp.bfloat16, jnp.float32
    x_at, t_at = lax.axis_index("heads"), lax.axis_index("team")
    z_at, y_at = lax.axis_index("z"), lax.axis_index("y")
    runs = run_index.reshape(T, Z, Y)
    own_run = lax.dynamic_index_in_dim(run_index, (t_at * Z + z_at) * Y + y_at, 0)
    local = x_at * PIECE + jnp.arange(PIECE, dtype=jnp.int32)
    early_at = own_run * HALF + local
    late_at = (2 * SLOTS - 1 - own_run) * HALF + local - HALF
    pos = jnp.where(local < HALF, early_at, late_at)
    angles = pos.astype(f32)[:, None] * inverse_freqs(HD)[None, :]
    cosine, sine = jnp.cos(angles)[:, None, :], jnp.sin(angles)[:, None, :]
    rot_q = rotate(queries[0].astype(f32), cosine, sine)
    rot_k = rotate(keys[0].astype(f32), cosine, sine)
    n_g = keys.shape[2]
    packed = jnp.concatenate(
        [rot_q.reshape(PIECE, n_g, GROUP, HD), rot_k[:, :, None], values[0][:, :, None]], axis=2
    )
    packed = packed.transpose(1, 2, 0, 3).reshape(n_g, (GROUP + 2) * PIECE, HD)
    mine = lax.all_to_all(packed, ("heads", "team"), split_axis=0, concat_axis=0, tiled=True)
    q_own = mine[:, :Q_ROWS].reshape(1, X * T * Q_ROWS, HD)
    kv_own = mine[:, Q_ROWS:].reshape(X * T * 2 * PIECE, HD)
    q_all = lax.all_to_all(
        jnp.broadcast_to(q_own, (Y,) + q_own.shape[1:]), "y", split_axis=0, concat_axis=0, tiled=True
    )
    kv_all = lax.all_gather(kv_own, "z", axis=0, tiled=False)
    q_run = lax.dynamic_index_in_dim(runs, z_at, 1, keepdims=False).reshape(T * Y)
    k_run = lax.dynamic_index_in_dim(runs, y_at, 2, keepdims=False).reshape(T * Z)
    smem = pl.BlockSpec(memory_space=pltpu.SMEM)
    vmem = pl.BlockSpec(memory_space=pltpu.VMEM)
    partial = pl.pallas_call(
        attend_kernel,
        out_shape=jax.ShapeDtypeStruct((T, Y, MSG, LANES), bf),
        in_specs=[smem, smem, vmem, vmem],
        out_specs=vmem,
        scratch_shapes=[
            pltpu.VMEM((2 * KEYS, HD), bf),
            pltpu.VMEM((HD, 2 * KEYS), bf),
            pltpu.VMEM((2 * KEYS, HD), jnp.int32),
        ],
        name="attend",
    )(
        q_run,
        k_run,
        q_all.reshape(Y, X, T, Q_ROWS, HD),
        kv_all.reshape(Z, X, T, 2, PIECE, HD),
    )
    parts = lax.all_to_all(
        partial.reshape(T * Y, MSG, LANES), ("team", "y"), split_axis=0, concat_axis=0, tiled=True
    )
    out = pl.pallas_call(
        combine_kernel,
        out_shape=jax.ShapeDtypeStruct((T * GROUP, 2 * HALF, HD), bf),
        in_specs=[vmem],
        out_specs=vmem,
        name="combine",
    )(parts.reshape(T, Y, MSG, LANES))
    return out.transpose(1, 0, 2)


def solution(mesh):
    split = Mesh(mesh.devices.reshape(X, T, Z, Y), ("heads", "team", "z", "y"))
    spec = P("heads", ("team", "z", "y"), None, None)
    return jax.shard_map(
        per_device,
        mesh=split,
        in_specs=(spec, spec, spec, P()),
        out_specs=P(("team", "z", "y"), "heads", None),
        check_vma=False,
    )
```

```python
import math

import jax
import jax.numpy as jnp
from jax import lax
from jax.experimental import pallas as pl
from jax.experimental.pallas import tpu as pltpu
from jax.sharding import Mesh, PartitionSpec as P

mask_floor = -1e30
rope_theta = 500000.0
rope_factor = 8.0
low_factor = 1.0
high_factor = 4.0
initial_context = 8192.0

X, T, Z, Y = 4, 2, 12, 8
PIECE = 16
HALF = 32
GROUP = 4
HD = 128
SLOTS = T * Z * Y
Q_ROWS = GROUP * PIECE
KEYS = Z * T * 2 * PIECE
LANES = 2 * Q_ROWS
MSG = 2 * HD + 16
CHUNK = 128
PRODUCE_FIRST = 1
LOG2_SCALE = HD ** -0.5 * math.log2(math.e)


def inverse_freqs(head_width):
    half_width = head_width // 2
    counter = jnp.arange(half_width, dtype=jnp.float32)
    base_freq = 1.0 / rope_theta ** (2.0 * counter / head_width)
    wavelength = 2.0 * jnp.pi / base_freq
    smooth = (initial_context / wavelength - low_factor) / (high_factor - low_factor)
    blended = (1.0 - smooth) * base_freq / rope_factor + smooth * base_freq
    middle = jnp.where(wavelength > initial_context / low_factor, base_freq / rope_factor, blended)
    return jnp.where(wavelength < initial_context / high_factor, base_freq, middle)


def pack_kernel(run_ref, freq_ref, q_ref, k_ref, v_ref, o_ref):
    f32 = jnp.float32
    x_at, t_at = lax.axis_index("heads"), lax.axis_index("team")
    z_at, y_at = lax.axis_index("z"), lax.axis_index("y")
    run = run_ref[(t_at * Z + z_at) * Y + y_at]
    base = jnp.where(x_at < 2, run * HALF, (2 * SLOTS - 1 - run) * HALF - HALF) + x_at * PIECE
    pos = lax.broadcasted_iota(jnp.int32, (PIECE, HD), 0) + base
    angles = pos.astype(f32) * freq_ref[...]
    cosine = jnp.cos(angles)[:, None, :]
    flip = jnp.where(lax.broadcasted_iota(jnp.int32, (PIECE, HD), 1) < HD // 2, -1.0, 1.0)
    sine = (jnp.sin(angles) * flip)[:, None, :]

    def turned(ref):
        x = ref[0].astype(f32)
        y = x * cosine + jnp.roll(x, HD // 2, axis=-1) * sine
        return jnp.swapaxes(y, 0, 1).astype(jnp.bfloat16)

    n_g = k_ref.shape[2]
    q = turned(q_ref).reshape(n_g, GROUP * PIECE, HD)
    o_ref[:, :Q_ROWS, :] = q
    o_ref[:, Q_ROWS : Q_ROWS + PIECE, :] = turned(k_ref)
    v = jnp.swapaxes(v_ref[0].astype(f32), 0, 1).astype(jnp.bfloat16)
    o_ref[:, Q_ROWS + PIECE :, :] = v


def attend_kernel(q_run, k_run, q_ref, kv_ref, o_ref, k_s, vt_s, kpos_s, se_s, sl_s, w_s):
    bf, f32 = jnp.bfloat16, jnp.float32
    for half in range(2):
        picked = kv_ref[:, 2 * half : 2 * half + 2]
        rows = slice(half * KEYS, (half + 1) * KEYS)
        k_s[rows, :] = picked[:, :, :, 0].reshape(KEYS, HD)
        vt_s[:, rows] = picked[:, :, :, 1].reshape(KEYS, HD).T
    row = lax.broadcasted_iota(jnp.int32, (PIECE, HD), 0)
    for z in range(Z):
        for x in range(4):
            for t in range(T):
                run = k_run[t * Z + z]
                base = run * HALF if x < 2 else (2 * SLOTS - 1 - run) * HALF
                at = (x // 2) * KEYS + ((z * 2 + x % 2) * T + t) * PIECE
                kpos_s[at : at + PIECE, :] = row + (base + (x % 2) * PIECE)
    lane = lax.broadcasted_iota(jnp.int32, (1, LANES), 1)
    local = (lane // Q_ROWS) * PIECE + lane % PIECE

    counts = (KEYS, 2 * KEYS)
    free = (0, KEYS)

    def tile(kind, y):
        return jnp.concatenate(
            [q_ref[y, 2 * kind + x, t] for t in range(T) for x in range(2)], axis=0
        )

    def q_pos(kind, y):
        runs = [q_run[t * Y + y] for t in range(T)]
        bases = [(2 * SLOTS - 1 - r) * HALF if kind else r * HALF for r in runs]
        return jnp.concatenate([local + b for b in bases], axis=1)

    def produce(kind, y, s_ref):
        q_tile, pos, top = tile(kind, y), q_pos(kind, y), None
        for at in range(0, counts[kind], CHUNK):
            rows = slice(at, at + CHUNK)
            s = lax.dot_general(
                k_s[rows, :], q_tile, (((1,), (1,)), ((), ())), preferred_element_type=f32
            )
            if at >= free[kind]:
                kp = kpos_s[rows, :]
                s = jnp.where(jnp.concatenate([kp, kp], axis=1) <= pos, s, mask_floor)
            s_ref[rows, :] = s
            best = jnp.max(s.reshape(CHUNK // 8, 8, 2 * LANES), axis=0)
            top = best if top is None else jnp.maximum(top, best)
            yield None
        yield jnp.max(top, axis=0, keepdims=True)

    def consume(kind, y, s_ref, top):
        total = jnp.zeros((8, 2 * LANES), f32)
        for at in range(0, counts[kind], CHUNK):
            rows = slice(at, at + CHUNK)
            w = jnp.exp2((s_ref[rows, :] - top) * LOG2_SCALE)
            total = total + jnp.sum(w.reshape(CHUNK // 8, 8, 2 * LANES), axis=0)
            w_s[kind, rows, :] = w.astype(bf)
            yield None
        total = jnp.sum(total, axis=0, keepdims=True)
        n = counts[kind]
        o = lax.dot_general(
            vt_s[:, :n], w_s[kind, :n, :], (((1,), (0,)), ((), ())), preferred_element_type=f32
        )
        o = (o * (1.0 / total)).astype(bf)
        lse = top * LOG2_SCALE + jnp.log2(total)
        hi = lse.astype(bf).astype(f32)
        mid = (lse - hi).astype(bf).astype(f32)
        low = lse - hi - mid
        pad = jnp.zeros((5, 2 * LANES), f32)
        stats = jnp.concatenate([hi, mid, low, pad], axis=0).astype(bf)
        for t in range(T):
            cols = slice(t * LANES, (t + 1) * LANES)
            o_ref[t, y, kind * HD : (kind + 1) * HD, :] = o[:, cols]
            o_ref[t, y, 2 * HD + 8 * kind : 2 * HD + 8 * kind + 8, :] = stats[:, cols]
        yield None

    def together(make, use):
        top, left = None, True
        ratio = PRODUCE_FIRST
        while left:
            left = False
            for _ in range(ratio):
                for got in make:
                    left = True
                    top = got if got is not None else top
                    break
            for _ in use:
                left = True
                break
        return top

    def only(make):
        top = None
        for got in make:
            top = got if got is not None else top
        return top

    def step(y, top_e):
        top_l = together(produce(1, y, sl_s), consume(0, y, se_s, top_e))
        after = jnp.minimum(y + 1, Y - 1)
        return together(produce(0, after, se_s), consume(1, y, sl_s, top_l))

    lax.fori_loop(0, Y, step, only(produce(0, 0, se_s)))


def combine_kernel(r_ref, o_ref):
    f32 = jnp.float32
    for half in range(2):
        heads = []
        for t in range(T):
            lse = []
            for y in range(Y):
                st = r_ref[t, y, 2 * HD + 8 * half : 2 * HD + 8 * half + 8, :].astype(f32)
                at = 0
                lse.append(st[at : at + 1] + st[at + 1 : at + 2] + st[at + 2 : at + 3])
            top = lse[0]
            for v in lse[1:]:
                top = jnp.maximum(top, v)
            ws = [jnp.exp2(v - top) for v in lse]
            total = ws[0]
            for v in ws[1:]:
                total = total + v
            acc = jnp.zeros((HD, LANES), f32)
            for y in range(Y):
                acc = acc + r_ref[t, y, half * HD : (half + 1) * HD, :].astype(f32) * ws[y]
            heads.append((acc * (1.0 / total)).T)
        for p in range(2):
            block = jnp.stack(
                [
                    heads[t][p * Q_ROWS + j * PIECE : p * Q_ROWS + (j + 1) * PIECE]
                    for t in range(T)
                    for j in range(GROUP)
                ],
                axis=0,
            )
            at = half * HALF + p * PIECE
            o_ref[at : at + PIECE] = jnp.swapaxes(block, 0, 1).astype(jnp.bfloat16)


def per_device(queries, keys, values, run_index):
    bf, f32 = jnp.bfloat16, jnp.float32
    z_at, y_at = lax.axis_index("z"), lax.axis_index("y")
    runs = run_index.reshape(T, Z, Y)
    smem = pl.BlockSpec(memory_space=pltpu.SMEM)
    vmem = pl.BlockSpec(memory_space=pltpu.VMEM)
    freqs = inverse_freqs(HD)
    packed = pl.pallas_call(
        pack_kernel,
        out_shape=jax.ShapeDtypeStruct((X * T, (GROUP + 2) * PIECE, HD), bf),
        in_specs=[smem, vmem, vmem, vmem, vmem],
        out_specs=vmem,
        compiler_params=pltpu.CompilerParams(vmem_limit_bytes=8 << 20),
        name="pack",
    )(run_index, jnp.concatenate([freqs, freqs])[None, :], queries, keys, values)
    mine = lax.all_to_all(packed, ("heads", "team"), split_axis=0, concat_axis=0, tiled=True)
    q_own = mine[:, :Q_ROWS].reshape(1, X * T * Q_ROWS, HD)
    kv_own = mine[:, Q_ROWS:].reshape(X * T * 2 * PIECE, HD)
    q_all = lax.all_to_all(
        jnp.broadcast_to(q_own, (Y,) + q_own.shape[1:]), "y", split_axis=0, concat_axis=0, tiled=True
    )
    kv_all = lax.all_gather(kv_own, "z", axis=0, tiled=False)
    q_run = lax.dynamic_index_in_dim(runs, z_at, 1, keepdims=False).reshape(T * Y)
    k_run = lax.dynamic_index_in_dim(runs, y_at, 2, keepdims=False).reshape(T * Z)
    partial = pl.pallas_call(
        attend_kernel,
        out_shape=jax.ShapeDtypeStruct((T, Y, MSG, LANES), bf),
        in_specs=[smem, smem, vmem, vmem],
        out_specs=vmem,
        scratch_shapes=[
            pltpu.VMEM((2 * KEYS, HD), bf),
            pltpu.VMEM((HD, 2 * KEYS), bf),
            pltpu.VMEM((2 * KEYS, HD), jnp.int32),
            pltpu.VMEM((KEYS, 2 * LANES), f32),
            pltpu.VMEM((2 * KEYS, 2 * LANES), f32),
            pltpu.VMEM((2, 2 * KEYS, 2 * LANES), bf),
        ],
        compiler_params=pltpu.CompilerParams(vmem_limit_bytes=24 << 20),
        name="attend",
    )(
        q_run,
        k_run,
        q_all.reshape(Y, X, T, Q_ROWS, HD),
        kv_all.reshape(Z, X, T, 2, PIECE, HD),
    )
    parts = lax.all_to_all(
        partial.reshape(T * Y, MSG, LANES), ("team", "y"), split_axis=0, concat_axis=0, tiled=True
    )
    return pl.pallas_call(
        combine_kernel,
        out_shape=jax.ShapeDtypeStruct((2 * HALF, T * GROUP, HD), bf),
        in_specs=[vmem],
        out_specs=vmem,
        compiler_params=pltpu.CompilerParams(vmem_limit_bytes=8 << 20),
        name="combine",
    )(parts.reshape(T, Y, MSG, LANES))


def solution(mesh):
    split = Mesh(mesh.devices.reshape(X, T, Z, Y), ("heads", "team", "z", "y"))
    spec = P("heads", ("team", "z", "y"), None, None)
    return jax.shard_map(
        per_device,
        mesh=split,
        in_specs=(spec, spec, spec, P()),
        out_specs=P(("team", "z", "y"), "heads", None),
        check_vma=False,
    )
```

```python
import math

import jax
import jax.numpy as jnp
from jax import lax
from jax.experimental import pallas as pl
from jax.experimental.pallas import tpu as pltpu
from jax.sharding import Mesh, PartitionSpec as P

mask_floor = -1e30
rope_theta = 500000.0
rope_factor = 8.0
low_factor = 1.0
high_factor = 4.0
initial_context = 8192.0

X, T, Z, YH, YL = 4, 2, 12, 4, 2
Y = YH * YL
PIECE = 16
HALF = 32
GROUP = 4
HD = 128
SLOTS = T * Z * Y
Q_ROWS = GROUP * PIECE
PART = Z * YL * 2 * PIECE
KEYS = T * PART
LANES = 2 * Q_ROWS
MSG = 2 * HD + 16
CHUNK = 128
PRODUCE_FIRST = 1
LOG2_SCALE = HD ** -0.5 * math.log2(math.e)


def inverse_freqs(head_width):
    half_width = head_width // 2
    counter = jnp.arange(half_width, dtype=jnp.float32)
    base_freq = 1.0 / rope_theta ** (2.0 * counter / head_width)
    wavelength = 2.0 * jnp.pi / base_freq
    smooth = (initial_context / wavelength - low_factor) / (high_factor - low_factor)
    blended = (1.0 - smooth) * base_freq / rope_factor + smooth * base_freq
    middle = jnp.where(wavelength > initial_context / low_factor, base_freq / rope_factor, blended)
    return jnp.where(wavelength < initial_context / high_factor, base_freq, middle)


def pack_kernel(run_ref, freq_ref, q_ref, k_ref, v_ref, o_ref):
    f32 = jnp.float32
    x_at, t_at = lax.axis_index("heads"), lax.axis_index("team")
    z_at, y_at = lax.axis_index("z"), lax.axis_index("yh") * YL + lax.axis_index("yl")
    run = run_ref[(t_at * Z + z_at) * Y + y_at]
    base = jnp.where(x_at < 2, run * HALF, (2 * SLOTS - 1 - run) * HALF - HALF) + x_at * PIECE
    pos = lax.broadcasted_iota(jnp.int32, (PIECE, HD), 0) + base
    angles = pos.astype(f32) * freq_ref[...]
    cosine = jnp.cos(angles)[:, None, :]
    flip = jnp.where(lax.broadcasted_iota(jnp.int32, (PIECE, HD), 1) < HD // 2, -1.0, 1.0)
    sine = (jnp.sin(angles) * flip)[:, None, :]

    def turned(ref):
        x = ref[0].astype(f32)
        y = x * cosine + jnp.roll(x, HD // 2, axis=-1) * sine
        return jnp.swapaxes(y, 0, 1).astype(jnp.bfloat16)

    n_g = k_ref.shape[2]
    q = turned(q_ref).reshape(n_g, GROUP * PIECE, HD)
    o_ref[:, :Q_ROWS, :] = q
    o_ref[:, Q_ROWS : Q_ROWS + PIECE, :] = turned(k_ref)
    v = jnp.swapaxes(v_ref[0].astype(f32), 0, 1).astype(jnp.bfloat16)
    o_ref[:, Q_ROWS + PIECE :, :] = v


def attend_kernel(run_ref, q_ref, near_ref, far_ref, o_ref, k_s, vt_s, kpos_s, se_s, sl_s, w_s):
    bf, f32 = jnp.bfloat16, jnp.float32
    t_at, z_at, yh_at = lax.axis_index("team"), lax.axis_index("z"), lax.axis_index("yh")
    row = lax.broadcasted_iota(jnp.int32, (PIECE, HD), 0)
    for part, kv_ref in enumerate((near_ref, far_ref)):
        team = t_at if part == 0 else 1 - t_at
        for half in range(2):
            picked = kv_ref[:, 2 * half : 2 * half + 2]
            start = half * KEYS + part * PART
            rows = slice(start, start + PART)
            k_s[rows, :] = picked[:, :, :, 0].reshape(PART, HD)
            vt_s[:, rows] = picked[:, :, :, 1].reshape(PART, HD).T
            for z in range(Z):
                for yl in range(YL):
                    run = run_ref[((team * Z + z) * YH + yh_at) * YL + yl]
                    base = (2 * SLOTS - 1 - run) * HALF if half else run * HALF
                    for x in range(2):
                        at = start + ((z * 2 + x) * YL + yl) * PIECE
                        kpos_s[at : at + PIECE, :] = row + (base + x * PIECE)
    lane = lax.broadcasted_iota(jnp.int32, (1, LANES), 1)
    local = (lane // Q_ROWS) * PIECE + lane % PIECE

    counts = (KEYS, 2 * KEYS)
    free = (0, KEYS)

    def tile(kind, y):
        return jnp.concatenate(
            [q_ref[y, 2 * kind + x, t] for t in range(YL) for x in range(2)], axis=0
        )

    def q_pos(kind, y):
        runs = [run_ref[((t_at * Z + z_at) * YH + y) * YL + t] for t in range(YL)]
        bases = [(2 * SLOTS - 1 - r) * HALF if kind else r * HALF for r in runs]
        return jnp.concatenate([local + b for b in bases], axis=1)

    def produce(kind, y, s_ref):
        q_tile, pos, top = tile(kind, y), q_pos(kind, y), None
        for at in range(0, counts[kind], CHUNK):
            rows = slice(at, at + CHUNK)
            s = lax.dot_general(
                k_s[rows, :], q_tile, (((1,), (1,)), ((), ())), preferred_element_type=f32
            )
            if at >= free[kind]:
                kp = kpos_s[rows, :]
                s = jnp.where(jnp.concatenate([kp, kp], axis=1) <= pos, s, mask_floor)
            s_ref[rows, :] = s
            best = jnp.max(s.reshape(CHUNK // 8, 8, 2 * LANES), axis=0)
            top = best if top is None else jnp.maximum(top, best)
            yield None
        yield jnp.max(top, axis=0, keepdims=True)

    def consume(kind, y, s_ref, top):
        total = jnp.zeros((8, 2 * LANES), f32)
        for at in range(0, counts[kind], CHUNK):
            rows = slice(at, at + CHUNK)
            w = jnp.exp2((s_ref[rows, :] - top) * LOG2_SCALE)
            total = total + jnp.sum(w.reshape(CHUNK // 8, 8, 2 * LANES), axis=0)
            w_s[kind, rows, :] = w.astype(bf)
            yield None
        total = jnp.sum(total, axis=0, keepdims=True)
        n = counts[kind]
        o = lax.dot_general(
            vt_s[:, :n], w_s[kind, :n, :], (((1,), (0,)), ((), ())), preferred_element_type=f32
        )
        o = (o * (1.0 / total)).astype(bf)
        lse = top * LOG2_SCALE + jnp.log2(total)
        hi = lse.astype(bf).astype(f32)
        mid = (lse - hi).astype(bf).astype(f32)
        low = lse - hi - mid
        pad = jnp.zeros((5, 2 * LANES), f32)
        stats = jnp.concatenate([hi, mid, low, pad], axis=0).astype(bf)
        for t in range(YL):
            cols = slice(t * LANES, (t + 1) * LANES)
            o_ref[y, t, kind * HD : (kind + 1) * HD, :] = o[:, cols]
            o_ref[y, t, 2 * HD + 8 * kind : 2 * HD + 8 * kind + 8, :] = stats[:, cols]
        yield None

    def together(make, use):
        top, left = None, True
        ratio = PRODUCE_FIRST
        while left:
            left = False
            for _ in range(ratio):
                for got in make:
                    left = True
                    top = got if got is not None else top
                    break
            for _ in use:
                left = True
                break
        return top

    def only(make):
        top = None
        for got in make:
            top = got if got is not None else top
        return top

    def step(y, top_e):
        top_l = together(produce(1, y, sl_s), consume(0, y, se_s, top_e))
        after = jnp.minimum(y + 1, YH - 1)
        return together(produce(0, after, se_s), consume(1, y, sl_s, top_l))

    lax.fori_loop(0, YH, step, only(produce(0, 0, se_s)))


def combine_kernel(r_ref, o_ref):
    f32 = jnp.float32
    for half in range(2):
        heads = []
        for t in range(YL):
            lse = []
            for y in range(YH):
                st = r_ref[y, t, 2 * HD + 8 * half : 2 * HD + 8 * half + 8, :].astype(f32)
                at = 0
                lse.append(st[at : at + 1] + st[at + 1 : at + 2] + st[at + 2 : at + 3])
            top = lse[0]
            for v in lse[1:]:
                top = jnp.maximum(top, v)
            ws = [jnp.exp2(v - top) for v in lse]
            total = ws[0]
            for v in ws[1:]:
                total = total + v
            acc = jnp.zeros((HD, LANES), f32)
            for y in range(YH):
                acc = acc + r_ref[y, t, half * HD : (half + 1) * HD, :].astype(f32) * ws[y]
            heads.append((acc * (1.0 / total)).T)
        for p in range(2):
            block = jnp.stack(
                [
                    heads[t][p * Q_ROWS + j * PIECE : p * Q_ROWS + (j + 1) * PIECE]
                    for t in range(YL)
                    for j in range(GROUP)
                ],
                axis=0,
            )
            at = half * HALF + p * PIECE
            o_ref[at : at + PIECE] = jnp.swapaxes(block, 0, 1).astype(jnp.bfloat16)


def per_device(queries, keys, values, run_index):
    bf, f32 = jnp.bfloat16, jnp.float32
    smem = pl.BlockSpec(memory_space=pltpu.SMEM)
    vmem = pl.BlockSpec(memory_space=pltpu.VMEM)
    freqs = inverse_freqs(HD)
    packed = pl.pallas_call(
        pack_kernel,
        out_shape=jax.ShapeDtypeStruct((X * YL, (GROUP + 2) * PIECE, HD), bf),
        in_specs=[smem, vmem, vmem, vmem, vmem],
        out_specs=vmem,
        compiler_params=pltpu.CompilerParams(vmem_limit_bytes=8 << 20),
        name="pack",
    )(run_index, jnp.concatenate([freqs, freqs])[None, :], queries, keys, values)
    mine = lax.all_to_all(packed, ("heads", "yl"), split_axis=0, concat_axis=0, tiled=True)
    q_own = mine[:, :Q_ROWS].reshape(1, X * YL * Q_ROWS, HD)
    kv_own = mine[:, Q_ROWS:].reshape(X * YL * 2 * PIECE, HD)
    q_all = lax.all_to_all(
        jnp.broadcast_to(q_own, (YH,) + q_own.shape[1:]),
        "yh",
        split_axis=0,
        concat_axis=0,
        tiled=True,
    )
    near = lax.all_gather(kv_own, "z", axis=0, tiled=False)
    far = lax.ppermute(near, "team", [(0, 1), (1, 0)])
    kv_shape = (Z, X, YL, 2, PIECE, HD)
    partial = pl.pallas_call(
        attend_kernel,
        out_shape=jax.ShapeDtypeStruct((YH, YL, MSG, LANES), bf),
        in_specs=[smem, vmem, vmem, vmem],
        out_specs=vmem,
        scratch_shapes=[
            pltpu.VMEM((2 * KEYS, HD), bf),
            pltpu.VMEM((HD, 2 * KEYS), bf),
            pltpu.VMEM((2 * KEYS, HD), jnp.int32),
            pltpu.VMEM((KEYS, 2 * LANES), f32),
            pltpu.VMEM((2 * KEYS, 2 * LANES), f32),
            pltpu.VMEM((2, 2 * KEYS, 2 * LANES), bf),
        ],
        compiler_params=pltpu.CompilerParams(vmem_limit_bytes=24 << 20),
        name="attend",
    )(
        run_index,
        q_all.reshape(YH, X, YL, Q_ROWS, HD),
        near.reshape(kv_shape),
        far.reshape(kv_shape),
    )
    parts = lax.all_to_all(
        partial.reshape(Y, MSG, LANES), ("yh", "yl"), split_axis=0, concat_axis=0, tiled=True
    )
    return pl.pallas_call(
        combine_kernel,
        out_shape=jax.ShapeDtypeStruct((2 * HALF, YL * GROUP, HD), bf),
        in_specs=[vmem],
        out_specs=vmem,
        compiler_params=pltpu.CompilerParams(vmem_limit_bytes=8 << 20),
        name="combine",
    )(parts.reshape(YH, YL, MSG, LANES))


def solution(mesh):
    axes = ("heads", "team", "z", "yh", "yl")
    split = Mesh(mesh.devices.reshape(X, T, Z, YH, YL), axes)
    spec = P("heads", axes[1:], None, None)
    return jax.shard_map(
        per_device,
        mesh=split,
        in_specs=(spec, spec, spec, P()),
        out_specs=P(axes[1:], "heads", None),
        check_vma=False,
    )
```

```python
import math

import jax
import jax.numpy as jnp
from jax import lax
from jax.experimental import pallas as pl
from jax.experimental.pallas import tpu as pltpu
from jax.sharding import Mesh, PartitionSpec as P

mask_floor = -1e30
rope_theta = 500000.0
rope_factor = 8.0
low_factor = 1.0
high_factor = 4.0
initial_context = 8192.0

X, T, Z, YH, YL = 4, 2, 12, 4, 2
Y = YH * YL
PIECE = 16
HALF = 32
GROUP = 4
HD = 128
SLOTS = T * Z * Y
Q_ROWS = GROUP * PIECE
PART = Z * YL * 2 * PIECE
KEYS = T * PART
LANES = 2 * Q_ROWS
OWN = T * Z * YL
MSG = 2 * HD + 16
CHUNK = 1536
PRODUCE_FIRST = 1
LOG2_SCALE = HD ** -0.5 * math.log2(math.e)


def inverse_freqs(head_width):
    half_width = head_width // 2
    counter = jnp.arange(half_width, dtype=jnp.float32)
    base_freq = 1.0 / rope_theta ** (2.0 * counter / head_width)
    wavelength = 2.0 * jnp.pi / base_freq
    smooth = (initial_context / wavelength - low_factor) / (high_factor - low_factor)
    blended = (1.0 - smooth) * base_freq / rope_factor + smooth * base_freq
    middle = jnp.where(wavelength > initial_context / low_factor, base_freq / rope_factor, blended)
    return jnp.where(wavelength < initial_context / high_factor, base_freq, middle)


def pack_kernel(run_ref, freq_ref, q_hbm, k_hbm, v_hbm, o_ref, q_ref, k_ref, v_ref, sems):
    f32 = jnp.float32
    moves = [
        pltpu.make_async_copy(src.at[0], dst, sems.at[i])
        for i, (src, dst) in enumerate(((q_hbm, q_ref), (k_hbm, k_ref), (v_hbm, v_ref)))
    ]
    for move in moves:
        move.start()
    x_at, t_at = lax.axis_index("heads"), lax.axis_index("team")
    z_at, y_at = lax.axis_index("z"), lax.axis_index("yh") * YL + lax.axis_index("yl")
    run = run_ref[(t_at * Z + z_at) * Y + y_at]
    base = jnp.where(x_at < 2, run * HALF, (2 * SLOTS - 1 - run) * HALF - HALF) + x_at * PIECE
    pos = lax.broadcasted_iota(jnp.int32, (PIECE, HD), 0) + base
    angles = pos.astype(f32) * freq_ref[...]
    cosine = jnp.cos(angles)[:, None, :]
    flip = jnp.where(lax.broadcasted_iota(jnp.int32, (PIECE, HD), 1) < HD // 2, -1.0, 1.0)
    sine = (jnp.sin(angles) * flip)[:, None, :]

    def turned(ref):
        x = ref[...].astype(f32)
        y = x * cosine + jnp.roll(x, HD // 2, axis=-1) * sine
        return jnp.swapaxes(y, 0, 1).astype(jnp.bfloat16)

    for move in moves:
        move.wait()
    n_g = k_ref.shape[1]
    o_ref[:, :Q_ROWS, :] = turned(q_ref).reshape(n_g, GROUP * PIECE, HD)
    o_ref[:, Q_ROWS : Q_ROWS + PIECE, :] = turned(k_ref)
    v = jnp.swapaxes(v_ref[...].astype(f32), 0, 1).astype(jnp.bfloat16)
    o_ref[:, Q_ROWS + PIECE :, :] = v


def spread_kernel(mine_ref, q_ref, kv_ref):
    q = mine_ref[:, :Q_ROWS, :].reshape(X * YL * Q_ROWS, HD)
    for i in range(YH):
        q_ref[i] = q
    kv_ref[...] = mine_ref[:, Q_ROWS:, :].reshape(X * YL * 2 * PIECE, HD)


def attend_kernel(run_ref, q_ref, near_ref, far_ref, o_ref, k_s, vt_s, own_s, se_s, sl_s, w_s):
    bf, f32 = jnp.bfloat16, jnp.float32
    t_at, z_at, yh_at = lax.axis_index("team"), lax.axis_index("z"), lax.axis_index("yh")
    row = lax.broadcasted_iota(jnp.int32, (PIECE, HD), 0)
    col = lax.broadcasted_iota(jnp.int32, (PIECE, HD), 1)
    lane = lax.broadcasted_iota(jnp.int32, (1, HD), 1)
    k_runs = jnp.zeros((1, HD), jnp.int32)
    for part, kv_ref in enumerate((near_ref, far_ref)):
        team = t_at if part == 0 else 1 - t_at
        for half in range(2):
            picked = kv_ref[:, 2 * half : 2 * half + 2]
            start = half * KEYS + part * PART
            rows = slice(start, start + PART)
            k_s[rows, :HD] = picked[:, :, :, 0].reshape(PART, HD)
            vt_s[:, rows] = picked[:, :, :, 1].reshape(PART, HD).T
        for z in range(Z):
            for yl in range(YL):
                slot = (part * Z + z) * YL + yl
                run = run_ref[((team * Z + z) * YH + yh_at) * YL + yl]
                k_runs = jnp.where(lane == slot, run, k_runs)
                for x in range(2):
                    hot = col == slot
                    if part == 0:
                        first = jnp.where(z_at == z, OWN + yl * HALF + x * PIECE, HD)
                        hot = hot | (col == row + first)
                    hot = jnp.where(hot, 1.0, 0.0).astype(bf)
                    for half in range(2):
                        at = half * KEYS + part * PART + ((z * 2 + x) * YL + yl) * PIECE
                        k_s[at : at + PIECE, HD:] = hot
    q_row = lax.broadcasted_iota(jnp.int32, (LANES, HD), 0)
    q_local = (q_row // Q_ROWS) * PIECE + q_row % PIECE
    k_local = lax.broadcasted_iota(jnp.int32, (LANES, HD), 1) - OWN
    for yl in range(YL):
        after = k_local - yl * HALF
        hidden = (after > q_local) & (after < HALF)
        own_s[yl] = jnp.where(hidden, mask_floor, 0.0)

    counts = (KEYS, 2 * KEYS)
    free = (0, KEYS)

    def tile(kind, y):
        return jnp.concatenate(
            [q_ref[y, 2 * kind + x, t] for t in range(YL) for x in range(2)], axis=0
        )

    def bias(kind, y):
        own = jnp.where(y == yh_at, 1.0, 0.0)
        blocks = []
        for yl in range(YL):
            run = run_ref[((t_at * Z + z_at) * YH + y) * YL + yl]
            later = (k_runs < run) if kind else (k_runs > run)
            hidden = jnp.where(later & (lane < OWN), mask_floor, 0.0)
            blocks.append((own_s[yl] * own + hidden).astype(bf))
        return jnp.concatenate(blocks, axis=0)

    def produce(kind, y, s_ref):
        q_tile, top = tile(kind, y), None
        q_wide = jnp.concatenate([q_tile, bias(kind, y)], axis=1)
        for at in range(0, counts[kind], CHUNK):
            rows = slice(at, at + CHUNK)
            k, q = (k_s[rows, :], q_wide) if at >= free[kind] else (k_s[rows, :HD], q_tile)
            s = lax.dot_general(k, q, (((1,), (1,)), ((), ())), preferred_element_type=f32)
            s_ref[rows, :] = s
            best = jnp.max(s.reshape(CHUNK // 8, 8, 2 * LANES), axis=0)
            top = best if top is None else jnp.maximum(top, best)
            yield None
        yield jnp.max(top, axis=0, keepdims=True)

    def consume(kind, y, s_ref, top):
        total = jnp.zeros((8, 2 * LANES), f32)
        for at in range(0, counts[kind], CHUNK):
            rows = slice(at, at + CHUNK)
            w = jnp.exp2((s_ref[rows, :] - top) * LOG2_SCALE)
            total = total + jnp.sum(w.reshape(CHUNK // 8, 8, 2 * LANES), axis=0)
            w_s[kind, rows, :] = w.astype(bf)
            yield None
        total = jnp.sum(total, axis=0, keepdims=True)
        n = counts[kind]
        o = lax.dot_general(
            vt_s[:, :n], w_s[kind, :n, :], (((1,), (0,)), ((), ())), preferred_element_type=f32
        )
        o = (o * (1.0 / total)).astype(bf)
        lse = top * LOG2_SCALE + jnp.log2(total)
        hi = lse.astype(bf).astype(f32)
        mid = (lse - hi).astype(bf).astype(f32)
        low = lse - hi - mid
        pad = jnp.zeros((5, 2 * LANES), f32)
        stats = jnp.concatenate([hi, mid, low, pad], axis=0).astype(bf)
        for t in range(YL):
            cols = slice(t * LANES, (t + 1) * LANES)
            o_ref[y, t, kind * HD : (kind + 1) * HD, :] = o[:, cols]
            o_ref[y, t, 2 * HD + 8 * kind : 2 * HD + 8 * kind + 8, :] = stats[:, cols]
        yield None

    def together(make, use):
        top, left = None, True
        ratio = PRODUCE_FIRST
        while left:
            left = False
            for _ in range(ratio):
                for got in make:
                    left = True
                    top = got if got is not None else top
                    break
            for _ in use:
                left = True
                break
        return top

    def only(make):
        top = None
        for got in make:
            top = got if got is not None else top
        return top

    def step(y, top_e):
        top_l = together(produce(1, y, sl_s), consume(0, y, se_s, top_e))
        after = jnp.minimum(y + 1, YH - 1)
        return together(produce(0, after, se_s), consume(1, y, sl_s, top_l))

    lax.fori_loop(0, YH, step, only(produce(0, 0, se_s)))


def combine_kernel(r_ref, o_ref):
    f32 = jnp.float32
    for half in range(2):
        heads = []
        for t in range(YL):
            lse = []
            for y in range(YH):
                st = r_ref[y, t, 2 * HD + 8 * half : 2 * HD + 8 * half + 8, :].astype(f32)
                at = 0
                lse.append(st[at : at + 1] + st[at + 1 : at + 2] + st[at + 2 : at + 3])
            top = lse[0]
            for v in lse[1:]:
                top = jnp.maximum(top, v)
            ws = [jnp.exp2(v - top) for v in lse]
            total = ws[0]
            for v in ws[1:]:
                total = total + v
            acc = jnp.zeros((HD, LANES), f32)
            for y in range(YH):
                acc = acc + r_ref[y, t, half * HD : (half + 1) * HD, :].astype(f32) * ws[y]
            heads.append((acc * (1.0 / total)).T)
        for p in range(2):
            block = jnp.stack(
                [
                    heads[t][p * Q_ROWS + j * PIECE : p * Q_ROWS + (j + 1) * PIECE]
                    for t in range(YL)
                    for j in range(GROUP)
                ],
                axis=0,
            )
            at = half * HALF + p * PIECE
            o_ref[at : at + PIECE] = jnp.swapaxes(block, 0, 1).astype(jnp.bfloat16)


def per_device(queries, keys, values, run_index):
    bf, f32 = jnp.bfloat16, jnp.float32
    smem = pl.BlockSpec(memory_space=pltpu.SMEM)
    vmem = pl.BlockSpec(memory_space=pltpu.VMEM)
    hbm = pl.BlockSpec(memory_space=pltpu.HBM)
    freqs = inverse_freqs(HD)
    packed = pl.pallas_call(
        pack_kernel,
        out_shape=jax.ShapeDtypeStruct((X * YL, (GROUP + 2) * PIECE, HD), bf),
        in_specs=[smem, vmem, hbm, hbm, hbm],
        out_specs=vmem,
        scratch_shapes=[pltpu.VMEM(a.shape[1:], bf) for a in (queries, keys, values)]
        + [pltpu.SemaphoreType.DMA((3,))],
        compiler_params=pltpu.CompilerParams(vmem_limit_bytes=60 << 20),
        name="pack",
    )(run_index, jnp.concatenate([freqs, freqs])[None, :], queries, keys, values)
    mine = lax.all_to_all(packed, ("heads", "yl"), split_axis=0, concat_axis=0, tiled=True)
    q_own, kv_own = pl.pallas_call(
        spread_kernel,
        out_shape=(
            jax.ShapeDtypeStruct((YH, X * YL * Q_ROWS, HD), bf),
            jax.ShapeDtypeStruct((X * YL * 2 * PIECE, HD), bf),
        ),
        in_specs=[vmem],
        out_specs=(vmem, vmem),
        compiler_params=pltpu.CompilerParams(vmem_limit_bytes=8 << 20),
        name="spread",
    )(mine)
    q_all = lax.all_to_all(q_own, "yh", split_axis=0, concat_axis=0, tiled=True)
    near = lax.all_gather(kv_own, "z", axis=0, tiled=False)
    far = lax.ppermute(near, "team", [(0, 1), (1, 0)])
    kv_shape = (Z, X, YL, 2, PIECE, HD)
    partial = pl.pallas_call(
        attend_kernel,
        out_shape=jax.ShapeDtypeStruct((YH, YL, MSG, LANES), bf),
        in_specs=[smem, vmem, vmem, vmem],
        out_specs=vmem,
        scratch_shapes=[
            pltpu.VMEM((2 * KEYS, 2 * HD), bf),
            pltpu.VMEM((HD, 2 * KEYS), bf),
            pltpu.VMEM((YL, LANES, HD), f32),
            pltpu.VMEM((KEYS, 2 * LANES), f32),
            pltpu.VMEM((2 * KEYS, 2 * LANES), f32),
            pltpu.VMEM((2, 2 * KEYS, 2 * LANES), bf),
        ],
        compiler_params=pltpu.CompilerParams(vmem_limit_bytes=24 << 20),
        name="attend",
    )(
        run_index,
        q_all.reshape(YH, X, YL, Q_ROWS, HD),
        near.reshape(kv_shape),
        far.reshape(kv_shape),
    )
    parts = lax.all_to_all(
        partial.reshape(Y, MSG, LANES), ("yh", "yl"), split_axis=0, concat_axis=0, tiled=True
    )
    return pl.pallas_call(
        combine_kernel,
        out_shape=jax.ShapeDtypeStruct((2 * HALF, YL * GROUP, HD), bf),
        in_specs=[vmem],
        out_specs=vmem,
        compiler_params=pltpu.CompilerParams(vmem_limit_bytes=8 << 20),
        name="combine",
    )(parts.reshape(YH, YL, MSG, LANES))


def solution(mesh):
    axes = ("heads", "team", "z", "yh", "yl")
    split = Mesh(mesh.devices.reshape(X, T, Z, YH, YL), axes)
    spec = P("heads", axes[1:], None, None)
    return jax.shard_map(
        per_device,
        mesh=split,
        in_specs=(spec, spec, spec, P()),
        out_specs=P(axes[1:], "heads", None),
        check_vma=False,
    )
```

```python
import functools
import math

import jax
import jax.numpy as jnp
import numpy as np
from jax import lax
from jax.experimental import pallas as pl
from jax.experimental.pallas import tpu as pltpu
from jax.sharding import Mesh, PartitionSpec as P

mask_floor = -1e30
rope_theta = 500000.0
rope_factor = 8.0
low_factor = 1.0
high_factor = 4.0
initial_context = 8192.0

X, T, Z, YH, YL = 4, 2, 12, 4, 2
Y = YH * YL
PIECE = 16
HALF = 32
GROUP = 4
HD = 128
SLOTS = T * Z * Y
Q_ROWS = GROUP * PIECE
PART = Z * YL * 2 * PIECE
LANES = 2 * Q_ROWS
OWN = Z * YL
MSG = 2 * HD + 8
LOG2_SCALE = HD ** -0.5 * math.log2(math.e)


def inverse_freqs():
    counter = np.arange(HD // 2, dtype=np.float64)
    base_freq = 1.0 / rope_theta ** (2.0 * counter / HD)
    wavelength = 2.0 * np.pi / base_freq
    smooth = (initial_context / wavelength - low_factor) / (high_factor - low_factor)
    blended = (1.0 - smooth) * base_freq / rope_factor + smooth * base_freq
    middle = np.where(wavelength > initial_context / low_factor, base_freq / rope_factor, blended)
    freqs = np.where(wavelength < initial_context / high_factor, base_freq, middle)
    return np.concatenate([freqs, freqs])[None, :].astype(np.float32)


def pack_kernel(run_ref, freq_ref, q_hbm, k_hbm, v_hbm, o_ref, q_ref, k_ref, v_ref, sems):
    f32 = jnp.float32
    moves = [
        pltpu.make_async_copy(src.at[0], dst, sems.at[i])
        for i, (src, dst) in enumerate(((q_hbm, q_ref), (k_hbm, k_ref), (v_hbm, v_ref)))
    ]
    for move in moves:
        move.start()
    x_at, t_at = lax.axis_index("heads"), lax.axis_index("team")
    z_at, y_at = lax.axis_index("z"), lax.axis_index("yh") * YL + lax.axis_index("yl")
    run = run_ref[(t_at * Z + z_at) * Y + y_at]
    base = jnp.where(x_at < 2, run * HALF, (2 * SLOTS - 1 - run) * HALF - HALF) + x_at * PIECE
    pos = lax.broadcasted_iota(jnp.int32, (PIECE, HD), 0) + base
    angles = pos.astype(f32) * freq_ref[...]
    cosine = jnp.cos(angles)[:, None, :]
    flip = jnp.where(lax.broadcasted_iota(jnp.int32, (PIECE, HD), 1) < HD // 2, -1.0, 1.0)
    sine = (jnp.sin(angles) * flip)[:, None, :]

    def turned(ref):
        x = ref[...].astype(f32)
        y = x * cosine + jnp.roll(x, HD // 2, axis=-1) * sine
        return jnp.swapaxes(y, 0, 1).astype(jnp.bfloat16)

    for move in moves:
        move.wait()
    n_g = k_ref.shape[1]
    o_ref[:, :Q_ROWS, :] = turned(q_ref).reshape(n_g, GROUP * PIECE, HD)
    o_ref[:, Q_ROWS : Q_ROWS + PIECE, :] = turned(k_ref)
    v = jnp.swapaxes(v_ref[...].astype(f32), 0, 1).astype(jnp.bfloat16)
    o_ref[:, Q_ROWS + PIECE :, :] = v


def spread_kernel(mine_ref, q_ref, kv_ref):
    q = mine_ref[:, :Q_ROWS, :].reshape(X * YL * Q_ROWS, HD)
    for i in range(YH):
        q_ref[i] = q
    kv_ref[...] = mine_ref[:, Q_ROWS:, :].reshape(X * YL * 2 * PIECE, HD)


def attend_kernel(part, run_ref, q_ref, kv_ref, *refs):
    bf, f32 = jnp.bfloat16, jnp.float32
    if part == 0:
        acc_ref, st_ref, k_s, vt_s, se_s, sl_s, w_s, own_s = refs
    else:
        acc_ref, st_ref, o_ref, k_s, vt_s, se_s, sl_s, w_s = refs
    t_at, z_at, yh_at = lax.axis_index("team"), lax.axis_index("z"), lax.axis_index("yh")
    row = lax.broadcasted_iota(jnp.int32, (PIECE, HD), 0)
    col = lax.broadcasted_iota(jnp.int32, (PIECE, HD), 1)
    lane = lax.broadcasted_iota(jnp.int32, (1, HD), 1)
    k_runs = jnp.zeros((1, HD), jnp.int32)
    team = t_at if part == 0 else 1 - t_at
    for half in range(2):
        picked = kv_ref[:, 2 * half : 2 * half + 2]
        rows = slice(half * PART, (half + 1) * PART)
        k_s[rows, :HD] = picked[:, :, :, 0].reshape(PART, HD)
        vt_s[:, rows] = picked[:, :, :, 1].reshape(PART, HD).T
    for z in range(Z):
        for yl in range(YL):
            slot = z * YL + yl
            run = run_ref[((team * Z + z) * YH + yh_at) * YL + yl]
            k_runs = jnp.where(lane == slot, run, k_runs)
            for x in range(2):
                hot = col == slot
                if part == 0:
                    first = jnp.where(z_at == z, OWN + yl * HALF + x * PIECE, HD)
                    hot = hot | (col == row + first)
                hot = jnp.where(hot, 1.0, 0.0).astype(bf)
                for half in range(2):
                    at = half * PART + ((z * 2 + x) * YL + yl) * PIECE
                    k_s[at : at + PIECE, HD:] = hot
    if part == 0:
        q_row = lax.broadcasted_iota(jnp.int32, (LANES, HD), 0)
        q_local = (q_row // Q_ROWS) * PIECE + q_row % PIECE
        k_local = lax.broadcasted_iota(jnp.int32, (LANES, HD), 1) - OWN
        for yl in range(YL):
            after = k_local - yl * HALF
            hidden = (after > q_local) & (after < HALF)
            own_s[yl] = jnp.where(hidden, mask_floor, 0.0)

    def tile(kind, y):
        return jnp.concatenate(
            [q_ref[y, 2 * kind + x, t] for t in range(YL) for x in range(2)], axis=0
        )

    def bias(kind, y):
        blocks = []
        for yl in range(YL):
            run = run_ref[((t_at * Z + z_at) * YH + y) * YL + yl]
            later = (k_runs < run) if kind else (k_runs > run)
            hidden = jnp.where(later & (lane < OWN), mask_floor, 0.0)
            if part == 0:
                hidden = own_s[yl] * jnp.where(y == yh_at, 1.0, 0.0) + hidden
            blocks.append(jnp.broadcast_to(hidden, (LANES, HD)).astype(bf))
        return jnp.concatenate(blocks, axis=0)

    def produce(kind, y, s_ref):
        q_tile = tile(kind, y)
        q_wide = jnp.concatenate([q_tile, bias(kind, y)], axis=1)
        pieces = [(slice(kind * PART, (kind + 1) * PART), q_wide)]
        if kind:
            pieces.append((slice(0, PART), q_tile))
        top = None
        for rows, q in pieces:
            s = lax.dot_general(
                k_s[rows, : q.shape[1]], q, (((1,), (1,)), ((), ())), preferred_element_type=f32
            )
            s_ref[rows, :] = s
            best = jnp.max(s.reshape(PART // 8, 8, 2 * LANES), axis=0)
            top = best if top is None else jnp.maximum(top, best)
        return jnp.max(top, axis=0, keepdims=True)

    def consume(kind, y, s_ref, top):
        total = jnp.zeros((8, 2 * LANES), f32)
        n = (kind + 1) * PART
        for at in range(0, n, PART):
            rows = slice(at, at + PART)
            w = jnp.exp2((s_ref[rows, :] - top) * LOG2_SCALE)
            total = total + jnp.sum(w.reshape(PART // 8, 8, 2 * LANES), axis=0)
            w_s[kind, rows, :] = w.astype(bf)
        total = jnp.sum(total, axis=0, keepdims=True)
        o = lax.dot_general(
            vt_s[:, :n], w_s[kind, :n, :], (((1,), (0,)), ((), ())), preferred_element_type=f32
        )
        if part == 0:
            acc_ref[y, kind] = o
            st_ref[y, kind, 0:1, :] = top
            st_ref[y, kind, 1:2, :] = total
            return None
        before = st_ref[y, kind, 0:1, :]
        best = jnp.maximum(top, before)
        keep = jnp.exp2((before - best) * LOG2_SCALE)
        add = jnp.exp2((top - best) * LOG2_SCALE)
        total = total * add + st_ref[y, kind, 1:2, :] * keep
        scale = 1.0 / total
        o = (o * (add * scale) + acc_ref[y, kind] * (keep * scale)).astype(bf)
        for t in range(YL):
            cols = slice(t * LANES, (t + 1) * LANES)
            o_ref[y, t, kind * HD : (kind + 1) * HD, :] = o[:, cols]
        lse = best * LOG2_SCALE + jnp.log2(total)
        hi = lse.astype(bf).astype(f32)
        mid = (lse - hi).astype(bf).astype(f32)
        return [hi, mid, lse - hi - mid]

    def step(y, top_e):
        top_l = produce(1, y, sl_s)
        early = consume(0, y, se_s, top_e)
        top_e = produce(0, jnp.minimum(y + 1, YH - 1), se_s)
        late = consume(1, y, sl_s, top_l)
        if part == 1:
            pad = jnp.zeros((2, 2 * LANES), f32)
            stats = jnp.concatenate(early + late + [pad], axis=0).astype(bf)
            for t in range(YL):
                o_ref[y, t, 2 * HD :, :] = stats[:, t * LANES : (t + 1) * LANES]
        return top_e

    lax.fori_loop(0, YH, step, produce(0, 0, se_s))


def combine_kernel(r_ref, o_ref):
    f32 = jnp.float32
    for half in range(2):
        heads = []
        for t in range(YL):
            lse = []
            for y in range(YH):
                st = r_ref[y, t, 2 * HD :, :].astype(f32)
                at = 3 * half
                lse.append(st[at : at + 1] + st[at + 1 : at + 2] + st[at + 2 : at + 3])
            top = lse[0]
            for v in lse[1:]:
                top = jnp.maximum(top, v)
            ws = [jnp.exp2(v - top) for v in lse]
            total = ws[0]
            for v in ws[1:]:
                total = total + v
            acc = jnp.zeros((HD, LANES), f32)
            for y in range(YH):
                acc = acc + r_ref[y, t, half * HD : (half + 1) * HD, :].astype(f32) * ws[y]
            heads.append((acc * (1.0 / total)).T)
        for p in range(2):
            block = jnp.stack(
                [
                    heads[t][p * Q_ROWS + j * PIECE : p * Q_ROWS + (j + 1) * PIECE]
                    for t in range(YL)
                    for j in range(GROUP)
                ],
                axis=0,
            )
            at = half * HALF + p * PIECE
            o_ref[at : at + PIECE] = jnp.swapaxes(block, 0, 1).astype(jnp.bfloat16)


def per_device(queries, keys, values, run_index):
    bf, f32 = jnp.bfloat16, jnp.float32
    smem = pl.BlockSpec(memory_space=pltpu.SMEM)
    vmem = pl.BlockSpec(memory_space=pltpu.VMEM)
    hbm = pl.BlockSpec(memory_space=pltpu.HBM)
    packed = pl.pallas_call(
        pack_kernel,
        out_shape=jax.ShapeDtypeStruct((X * YL, (GROUP + 2) * PIECE, HD), bf),
        in_specs=[smem, vmem, hbm, hbm, hbm],
        out_specs=vmem,
        scratch_shapes=[pltpu.VMEM(a.shape[1:], bf) for a in (queries, keys, values)]
        + [pltpu.SemaphoreType.DMA((3,))],
        compiler_params=pltpu.CompilerParams(vmem_limit_bytes=60 << 20),
        name="pack",
    )(run_index, inverse_freqs(), queries, keys, values)
    mine = lax.all_to_all(packed, ("heads", "yl"), split_axis=0, concat_axis=0, tiled=True)
    q_own, kv_own = pl.pallas_call(
        spread_kernel,
        out_shape=(
            jax.ShapeDtypeStruct((YH, X * YL * Q_ROWS, HD), bf),
            jax.ShapeDtypeStruct((X * YL * 2 * PIECE, HD), bf),
        ),
        in_specs=[vmem],
        out_specs=(vmem, vmem),
        compiler_params=pltpu.CompilerParams(vmem_limit_bytes=8 << 20),
        name="spread",
    )(mine)
    q_all = lax.all_to_all(q_own, "yh", split_axis=0, concat_axis=0, tiled=True)
    near = lax.all_gather(kv_own, "z", axis=0, tiled=False)
    far = lax.ppermute(near, "team", [(0, 1), (1, 0)])
    kv_shape = (Z, X, YL, 2, PIECE, HD)
    q_all = q_all.reshape(YH, X, YL, Q_ROWS, HD)
    f32 = jnp.float32

    def attend(part, kv, *state):
        if part == 0:
            out = (
                jax.ShapeDtypeStruct((YH, 2, HD, 2 * LANES), f32),
                jax.ShapeDtypeStruct((YH, 2, 8, 2 * LANES), f32),
            )
        else:
            out = jax.ShapeDtypeStruct((YH, YL, MSG, LANES), bf)
        scratch = [
            pltpu.VMEM((2 * PART, 2 * HD), bf),
            pltpu.VMEM((HD, 2 * PART), bf),
            pltpu.VMEM((PART, 2 * LANES), f32),
            pltpu.VMEM((2 * PART, 2 * LANES), f32),
            pltpu.VMEM((2, 2 * PART, 2 * LANES), bf),
        ]
        return pl.pallas_call(
            functools.partial(attend_kernel, part),
            out_shape=out,
            in_specs=[smem, vmem, vmem] + [vmem] * len(state),
            out_specs=(vmem, vmem) if part == 0 else vmem,
            scratch_shapes=scratch + [pltpu.VMEM((YL, LANES, HD), f32)] * (part == 0),
            compiler_params=pltpu.CompilerParams(vmem_limit_bytes=20 << 20),
            name=("attend_near", "attend_far")[part],
        )(run_index, q_all, kv.reshape(kv_shape), *state)

    partial = attend(1, far, *attend(0, near))
    parts = lax.all_to_all(
        partial.reshape(Y, MSG, LANES), ("yh", "yl"), split_axis=0, concat_axis=0, tiled=True
    )
    return pl.pallas_call(
        combine_kernel,
        out_shape=jax.ShapeDtypeStruct((2 * HALF, YL * GROUP, HD), bf),
        in_specs=[vmem],
        out_specs=vmem,
        compiler_params=pltpu.CompilerParams(vmem_limit_bytes=8 << 20),
        name="combine",
    )(parts.reshape(YH, YL, MSG, LANES))


def solution(mesh):
    axes = ("heads", "team", "z", "yh", "yl")
    split = Mesh(mesh.devices.reshape(X, T, Z, YH, YL), axes)
    spec = P("heads", axes[1:], None, None)
    return jax.shard_map(
        per_device,
        mesh=split,
        in_specs=(spec, spec, spec, P()),
        out_specs=P(axes[1:], "heads", None),
        check_vma=False,
    )
```

```python
import functools
import math

import jax
import jax.numpy as jnp
import numpy as np
from jax import lax
from jax.experimental import pallas as pl
from jax.experimental.pallas import tpu as pltpu
from jax.sharding import Mesh, PartitionSpec as P

mask_floor = -1e30
rope_theta = 500000.0
rope_factor = 8.0
low_factor = 1.0
high_factor = 4.0
initial_context = 8192.0

X, T, Z, YH, YL = 4, 2, 12, 4, 2
Y = YH * YL
PIECE = 16
HALF = 32
GROUP = 4
HD = 128
SLOTS = T * Z * Y
Q_ROWS = GROUP * PIECE
PART = Z * YL * 2 * PIECE
LANES = 2 * Q_ROWS
OWN = Z * YL
MSG = 2 * HD + 8
LOG2_SCALE = HD ** -0.5 * math.log2(math.e)


def inverse_freqs():
    counter = np.arange(HD // 2, dtype=np.float64)
    base_freq = 1.0 / rope_theta ** (2.0 * counter / HD)
    wavelength = 2.0 * np.pi / base_freq
    smooth = (initial_context / wavelength - low_factor) / (high_factor - low_factor)
    blended = (1.0 - smooth) * base_freq / rope_factor + smooth * base_freq
    middle = np.where(wavelength > initial_context / low_factor, base_freq / rope_factor, blended)
    freqs = np.where(wavelength < initial_context / high_factor, base_freq, middle)
    return np.concatenate([freqs, freqs])[None, :].astype(np.float32)


def pack_kernel(
    run_hbm, freq_hbm, q_hbm, k_hbm, v_hbm, o_ref, run_ref, freq_ref, q_ref, k_ref, v_ref, sems
):
    f32 = jnp.float32
    pairs = (
        (run_hbm, run_ref),
        (freq_hbm, freq_ref),
        (q_hbm.at[0], q_ref),
        (k_hbm.at[0], k_ref),
        (v_hbm.at[0], v_ref),
    )
    moves = [pltpu.make_async_copy(a, b, sems.at[i]) for i, (a, b) in enumerate(pairs)]
    for move in moves:
        move.start()
    for move in moves[:2]:
        move.wait()
    x_at, t_at = lax.axis_index("heads"), lax.axis_index("team")
    z_at, y_at = lax.axis_index("z"), lax.axis_index("yh") * YL + lax.axis_index("yl")
    run = run_ref[(t_at * Z + z_at) * Y + y_at]
    base = jnp.where(x_at < 2, run * HALF, (2 * SLOTS - 1 - run) * HALF - HALF) + x_at * PIECE
    pos = lax.broadcasted_iota(jnp.int32, (PIECE, HD), 0) + base
    angles = pos.astype(f32) * freq_ref[...]
    cosine = jnp.cos(angles)[:, None, :]
    flip = jnp.where(lax.broadcasted_iota(jnp.int32, (PIECE, HD), 1) < HD // 2, -1.0, 1.0)
    sine = (jnp.sin(angles) * flip)[:, None, :]

    def turned(ref):
        x = ref[...].astype(f32)
        y = x * cosine + jnp.roll(x, HD // 2, axis=-1) * sine
        return jnp.swapaxes(y, 0, 1).astype(jnp.bfloat16)

    for move in moves[2:]:
        move.wait()
    n_g = k_ref.shape[1]
    o_ref[:, :Q_ROWS, :] = turned(q_ref).reshape(n_g, GROUP * PIECE, HD)
    o_ref[:, Q_ROWS : Q_ROWS + PIECE, :] = turned(k_ref)
    v = jnp.swapaxes(v_ref[...].astype(f32), 0, 1).astype(jnp.bfloat16)
    o_ref[:, Q_ROWS + PIECE :, :] = v


def spread_kernel(mine_ref, q_ref, kv_ref):
    q = mine_ref[:, :Q_ROWS, :].reshape(X * YL * Q_ROWS, HD)
    for i in range(YH):
        q_ref[i] = q
    kv_ref[...] = mine_ref[:, Q_ROWS:, :].reshape(X * YL * 2 * PIECE, HD)


def attend_kernel(part, run_ref, q_ref, kv_ref, *refs):
    bf, f32 = jnp.bfloat16, jnp.float32
    if part == 0:
        acc_ref, st_ref, k_s, vt_s, se_s, sl_s, w_s, own_s = refs
    else:
        acc_ref, st_ref, o_ref, k_s, vt_s, se_s, sl_s, w_s = refs
    t_at, z_at, yh_at = lax.axis_index("team"), lax.axis_index("z"), lax.axis_index("yh")
    row = lax.broadcasted_iota(jnp.int32, (PIECE, HD), 0)
    col = lax.broadcasted_iota(jnp.int32, (PIECE, HD), 1)
    lane = lax.broadcasted_iota(jnp.int32, (1, HD), 1)
    k_runs = jnp.zeros((1, HD), jnp.int32)
    team = t_at if part == 0 else 1 - t_at
    for half in range(2):
        picked = kv_ref[:, 2 * half : 2 * half + 2]
        rows = slice(half * PART, (half + 1) * PART)
        k_s[rows, :HD] = picked[:, :, :, 0].reshape(PART, HD)
        vt_s[:, rows] = picked[:, :, :, 1].reshape(PART, HD).T
    for z in range(Z):
        for yl in range(YL):
            slot = z * YL + yl
            run = run_ref[((team * Z + z) * YH + yh_at) * YL + yl]
            k_runs = jnp.where(lane == slot, run, k_runs)
            for x in range(2):
                hot = col == slot
                if part == 0:
                    first = jnp.where(z_at == z, OWN + yl * HALF + x * PIECE, HD)
                    hot = hot | (col == row + first)
                hot = jnp.where(hot, 1.0, 0.0).astype(bf)
                for half in range(2):
                    at = half * PART + ((z * 2 + x) * YL + yl) * PIECE
                    k_s[at : at + PIECE, HD:] = hot
    if part == 0:
        q_row = lax.broadcasted_iota(jnp.int32, (LANES, HD), 0)
        q_local = (q_row // Q_ROWS) * PIECE + q_row % PIECE
        k_local = lax.broadcasted_iota(jnp.int32, (LANES, HD), 1) - OWN
        for yl in range(YL):
            after = k_local - yl * HALF
            hidden = (after > q_local) & (after < HALF)
            own_s[yl] = jnp.where(hidden, mask_floor, 0.0)

    def tile(kind, y):
        return jnp.concatenate(
            [q_ref[y, 2 * kind + x, t] for t in range(YL) for x in range(2)], axis=0
        )

    def bias(kind, y):
        blocks = []
        for yl in range(YL):
            run = run_ref[((t_at * Z + z_at) * YH + y) * YL + yl]
            later = (k_runs < run) if kind else (k_runs > run)
            hidden = jnp.where(later & (lane < OWN), mask_floor, 0.0)
            if part == 0:
                hidden = own_s[yl] * jnp.where(y == yh_at, 1.0, 0.0) + hidden
            blocks.append(jnp.broadcast_to(hidden, (LANES, HD)).astype(bf))
        return jnp.concatenate(blocks, axis=0)

    def produce(kind, y, s_ref):
        q_tile = tile(kind, y)
        q_wide = jnp.concatenate([q_tile, bias(kind, y)], axis=1)
        pieces = [(slice(kind * PART, (kind + 1) * PART), q_wide)]
        if kind:
            pieces.append((slice(0, PART), q_tile))
        top = None
        for rows, q in pieces:
            s = lax.dot_general(
                k_s[rows, : q.shape[1]], q, (((1,), (1,)), ((), ())), preferred_element_type=f32
            )
            s_ref[rows, :] = s
            best = jnp.max(s.reshape(PART // 8, 8, 2 * LANES), axis=0)
            top = best if top is None else jnp.maximum(top, best)
        return jnp.max(top, axis=0, keepdims=True)

    def consume(kind, y, s_ref, top):
        total = jnp.zeros((8, 2 * LANES), f32)
        n = (kind + 1) * PART
        for at in range(0, n, PART):
            rows = slice(at, at + PART)
            w = jnp.exp2((s_ref[rows, :] - top) * LOG2_SCALE)
            total = total + jnp.sum(w.reshape(PART // 8, 8, 2 * LANES), axis=0)
            w_s[kind, rows, :] = w.astype(bf)
        total = jnp.sum(total, axis=0, keepdims=True)
        o = lax.dot_general(
            vt_s[:, :n], w_s[kind, :n, :], (((1,), (0,)), ((), ())), preferred_element_type=f32
        )
        if part == 0:
            acc_ref[y, kind] = o
            st_ref[y, kind, 0:1, :] = top
            st_ref[y, kind, 1:2, :] = total
            return None
        before = st_ref[y, kind, 0:1, :]
        best = jnp.maximum(top, before)
        keep = jnp.exp2((before - best) * LOG2_SCALE)
        add = jnp.exp2((top - best) * LOG2_SCALE)
        total = total * add + st_ref[y, kind, 1:2, :] * keep
        scale = 1.0 / total
        o = (o * (add * scale) + acc_ref[y, kind] * (keep * scale)).astype(bf)
        for t in range(YL):
            cols = slice(t * LANES, (t + 1) * LANES)
            o_ref[y, t, kind * HD : (kind + 1) * HD, :] = o[:, cols]
        lse = best * LOG2_SCALE + jnp.log2(total)
        hi = lse.astype(bf).astype(f32)
        mid = (lse - hi).astype(bf).astype(f32)
        return [hi, mid, lse - hi - mid]

    def step(y, top_e):
        top_l = produce(1, y, sl_s)
        early = consume(0, y, se_s, top_e)
        top_e = produce(0, jnp.minimum(y + 1, YH - 1), se_s)
        late = consume(1, y, sl_s, top_l)
        if part == 1:
            pad = jnp.zeros((2, 2 * LANES), f32)
            stats = jnp.concatenate(early + late + [pad], axis=0).astype(bf)
            for t in range(YL):
                o_ref[y, t, 2 * HD :, :] = stats[:, t * LANES : (t + 1) * LANES]
        return top_e

    lax.fori_loop(0, YH, step, produce(0, 0, se_s))


def combine_kernel(r_ref, o_ref):
    f32 = jnp.float32
    for half in range(2):
        heads = []
        for t in range(YL):
            lse = []
            for y in range(YH):
                st = r_ref[y, t, 2 * HD :, :].astype(f32)
                at = 3 * half
                lse.append(st[at : at + 1] + st[at + 1 : at + 2] + st[at + 2 : at + 3])
            top = lse[0]
            for v in lse[1:]:
                top = jnp.maximum(top, v)
            ws = [jnp.exp2(v - top) for v in lse]
            total = ws[0]
            for v in ws[1:]:
                total = total + v
            acc = jnp.zeros((HD, LANES), f32)
            for y in range(YH):
                acc = acc + r_ref[y, t, half * HD : (half + 1) * HD, :].astype(f32) * ws[y]
            heads.append((acc * (1.0 / total)).T)
        for p in range(2):
            block = jnp.stack(
                [
                    heads[t][p * Q_ROWS + j * PIECE : p * Q_ROWS + (j + 1) * PIECE]
                    for t in range(YL)
                    for j in range(GROUP)
                ],
                axis=0,
            )
            at = half * HALF + p * PIECE
            o_ref[at : at + PIECE] = jnp.swapaxes(block, 0, 1).astype(jnp.bfloat16)


def per_device(queries, keys, values, run_index):
    bf, f32 = jnp.bfloat16, jnp.float32
    smem = pl.BlockSpec(memory_space=pltpu.SMEM)
    vmem = pl.BlockSpec(memory_space=pltpu.VMEM)
    hbm = pl.BlockSpec(memory_space=pltpu.HBM)
    packed = pl.pallas_call(
        pack_kernel,
        out_shape=jax.ShapeDtypeStruct((X * YL, (GROUP + 2) * PIECE, HD), bf),
        in_specs=[hbm] * 5,
        out_specs=vmem,
        scratch_shapes=[pltpu.SMEM((SLOTS,), jnp.int32), pltpu.VMEM((1, HD), jnp.float32)]
        + [pltpu.VMEM(a.shape[1:], bf) for a in (queries, keys, values)]
        + [pltpu.SemaphoreType.DMA((5,))],
        compiler_params=pltpu.CompilerParams(vmem_limit_bytes=60 << 20),
        name="pack",
    )(run_index, inverse_freqs(), queries, keys, values)
    mine = lax.all_to_all(packed, ("heads", "yl"), split_axis=0, concat_axis=0, tiled=True)
    q_own, kv_own = pl.pallas_call(
        spread_kernel,
        out_shape=(
            jax.ShapeDtypeStruct((YH, X * YL * Q_ROWS, HD), bf),
            jax.ShapeDtypeStruct((X * YL * 2 * PIECE, HD), bf),
        ),
        in_specs=[vmem],
        out_specs=(vmem, vmem),
        compiler_params=pltpu.CompilerParams(vmem_limit_bytes=8 << 20),
        name="spread",
    )(mine)
    q_all = lax.all_to_all(q_own, "yh", split_axis=0, concat_axis=0, tiled=True)
    near = lax.all_gather(kv_own, "z", axis=0, tiled=False)
    far = lax.ppermute(near, "team", [(0, 1), (1, 0)])
    kv_shape = (Z, X, YL, 2, PIECE, HD)
    q_all = q_all.reshape(YH, X, YL, Q_ROWS, HD)
    f32 = jnp.float32

    def attend(part, kv, *state):
        if part == 0:
            out = (
                jax.ShapeDtypeStruct((YH, 2, HD, 2 * LANES), f32),
                jax.ShapeDtypeStruct((YH, 2, 8, 2 * LANES), f32),
            )
        else:
            out = jax.ShapeDtypeStruct((YH, YL, MSG, LANES), bf)
        scratch = [
            pltpu.VMEM((2 * PART, 2 * HD), bf),
            pltpu.VMEM((HD, 2 * PART), bf),
            pltpu.VMEM((PART, 2 * LANES), f32),
            pltpu.VMEM((2 * PART, 2 * LANES), f32),
            pltpu.VMEM((2, 2 * PART, 2 * LANES), bf),
        ]
        return pl.pallas_call(
            functools.partial(attend_kernel, part),
            out_shape=out,
            in_specs=[smem, vmem, vmem] + [vmem] * len(state),
            out_specs=(vmem, vmem) if part == 0 else vmem,
            scratch_shapes=scratch + [pltpu.VMEM((YL, LANES, HD), f32)] * (part == 0),
            compiler_params=pltpu.CompilerParams(vmem_limit_bytes=20 << 20),
            name=("attend_near", "attend_far")[part],
        )(run_index, q_all, kv.reshape(kv_shape), *state)

    partial = attend(1, far, *attend(0, near))
    parts = lax.all_to_all(
        partial.reshape(Y, MSG, LANES), ("yh", "yl"), split_axis=0, concat_axis=0, tiled=True
    )
    return pl.pallas_call(
        combine_kernel,
        out_shape=jax.ShapeDtypeStruct((2 * HALF, YL * GROUP, HD), bf),
        in_specs=[vmem],
        out_specs=vmem,
        compiler_params=pltpu.CompilerParams(vmem_limit_bytes=8 << 20),
        name="combine",
    )(parts.reshape(YH, YL, MSG, LANES))


def solution(mesh):
    axes = ("heads", "team", "z", "yh", "yl")
    split = Mesh(mesh.devices.reshape(X, T, Z, YH, YL), axes)
    spec = P("heads", axes[1:], None, None)
    return jax.shard_map(
        per_device,
        mesh=split,
        in_specs=(spec, spec, spec, P()),
        out_specs=P(axes[1:], "heads", None),
        check_vma=False,
    )
```

```python
import functools
import math

import jax
import jax.numpy as jnp
import numpy as np
from jax import lax
from jax.experimental import pallas as pl
from jax.experimental.pallas import tpu as pltpu
from jax.sharding import Mesh, PartitionSpec as P

mask_floor = -1e30
rope_theta = 500000.0
rope_factor = 8.0
low_factor = 1.0
high_factor = 4.0
initial_context = 8192.0

X, T, Z, YH, YL = 4, 2, 12, 4, 2
Y = YH * YL
PIECE = 16
HALF = 32
GROUP = 4
HD = 128
SLOTS = T * Z * Y
Q_ROWS = GROUP * PIECE
PART = Z * YL * 2 * PIECE
LANES = 2 * Q_ROWS
OWN = Z * YL
MSG = 2 * HD + 8
LOG2_SCALE = HD ** -0.5 * math.log2(math.e)


def inverse_freqs():
    counter = np.arange(HD // 2, dtype=np.float64)
    base_freq = 1.0 / rope_theta ** (2.0 * counter / HD)
    wavelength = 2.0 * np.pi / base_freq
    smooth = (initial_context / wavelength - low_factor) / (high_factor - low_factor)
    blended = (1.0 - smooth) * base_freq / rope_factor + smooth * base_freq
    middle = np.where(wavelength > initial_context / low_factor, base_freq / rope_factor, blended)
    freqs = np.where(wavelength < initial_context / high_factor, base_freq, middle)
    return np.concatenate([freqs, freqs])[None, :].astype(np.float32)


def pack_kernel(
    run_hbm, freq_hbm, q_hbm, k_hbm, v_hbm, o_ref, run_ref, freq_ref, q_ref, k_ref, v_ref, sems
):
    f32 = jnp.float32
    pairs = (
        (run_hbm, run_ref),
        (freq_hbm, freq_ref),
        (q_hbm.at[0], q_ref),
        (k_hbm.at[0], k_ref),
        (v_hbm.at[0], v_ref),
    )
    moves = [pltpu.make_async_copy(a, b, sems.at[i]) for i, (a, b) in enumerate(pairs)]
    for move in moves:
        move.start()
    for move in moves[:2]:
        move.wait()
    x_at, t_at = lax.axis_index("heads"), lax.axis_index("team")
    z_at, y_at = lax.axis_index("z"), lax.axis_index("yh") * YL + lax.axis_index("yl")
    run = run_ref[(t_at * Z + z_at) * Y + y_at]
    base = jnp.where(x_at < 2, run * HALF, (2 * SLOTS - 1 - run) * HALF - HALF) + x_at * PIECE
    pos = lax.broadcasted_iota(jnp.int32, (PIECE, HD), 0) + base
    angles = pos.astype(f32) * freq_ref[...]
    cosine = jnp.cos(angles)[:, None, :]
    flip = jnp.where(lax.broadcasted_iota(jnp.int32, (PIECE, HD), 1) < HD // 2, -1.0, 1.0)
    sine = (jnp.sin(angles) * flip)[:, None, :]

    def turned(ref):
        x = ref[...].astype(f32)
        y = x * cosine + jnp.roll(x, HD // 2, axis=-1) * sine
        return jnp.swapaxes(y, 0, 1).astype(jnp.bfloat16)

    for move in moves[2:]:
        move.wait()
    n_g = k_ref.shape[1]
    o_ref[:, :Q_ROWS, :] = turned(q_ref).reshape(n_g, GROUP * PIECE, HD)
    o_ref[:, Q_ROWS : Q_ROWS + PIECE, :] = turned(k_ref)
    v = jnp.swapaxes(v_ref[...].astype(f32), 0, 1).astype(jnp.bfloat16)
    o_ref[:, Q_ROWS + PIECE :, :] = v


def spread_kernel(mine_ref, q_ref, kv_ref):
    q = mine_ref[:, :Q_ROWS, :].reshape(X * YL * Q_ROWS, HD)
    for i in range(YH):
        q_ref[i] = q
    kv_ref[...] = mine_ref[:, Q_ROWS:, :].reshape(X * YL * 2 * PIECE, HD)


def attend_kernel(part, run_hbm, q_ref, kv_ref, *refs):
    bf, f32 = jnp.bfloat16, jnp.float32
    *refs, run_ref, sem = refs
    fetch = pltpu.make_async_copy(run_hbm, run_ref, sem)
    fetch.start()
    if part == 0:
        acc_ref, st_ref, k_s, vt_s, se_s, sl_s, w_s, own_s = refs
    else:
        acc_ref, st_ref, o_ref, k_s, vt_s, se_s, sl_s, w_s = refs
    t_at, z_at, yh_at = lax.axis_index("team"), lax.axis_index("z"), lax.axis_index("yh")
    row = lax.broadcasted_iota(jnp.int32, (PIECE, HD), 0)
    col = lax.broadcasted_iota(jnp.int32, (PIECE, HD), 1)
    lane = lax.broadcasted_iota(jnp.int32, (1, HD), 1)
    k_runs = jnp.zeros((1, HD), jnp.int32)
    team = t_at if part == 0 else 1 - t_at
    for half in range(2):
        picked = kv_ref[:, 2 * half : 2 * half + 2]
        rows = slice(half * PART, (half + 1) * PART)
        k_s[rows, :HD] = picked[:, :, :, 0].reshape(PART, HD)
        vt_s[:, rows] = picked[:, :, :, 1].reshape(PART, HD).T
    fetch.wait()
    for z in range(Z):
        for yl in range(YL):
            slot = z * YL + yl
            run = run_ref[((team * Z + z) * YH + yh_at) * YL + yl]
            k_runs = jnp.where(lane == slot, run, k_runs)
            for x in range(2):
                hot = col == slot
                if part == 0:
                    first = jnp.where(z_at == z, OWN + yl * HALF + x * PIECE, HD)
                    hot = hot | (col == row + first)
                hot = jnp.where(hot, 1.0, 0.0).astype(bf)
                for half in range(2):
                    at = half * PART + ((z * 2 + x) * YL + yl) * PIECE
                    k_s[at : at + PIECE, HD:] = hot
    if part == 0:
        q_row = lax.broadcasted_iota(jnp.int32, (LANES, HD), 0)
        q_local = (q_row // Q_ROWS) * PIECE + q_row % PIECE
        k_local = lax.broadcasted_iota(jnp.int32, (LANES, HD), 1) - OWN
        for yl in range(YL):
            after = k_local - yl * HALF
            hidden = (after > q_local) & (after < HALF)
            own_s[yl] = jnp.where(hidden, mask_floor, 0.0)

    def tile(kind, y):
        return jnp.concatenate(
            [q_ref[y, 2 * kind + x, t] for t in range(YL) for x in range(2)], axis=0
        )

    def bias(kind, y):
        blocks = []
        for yl in range(YL):
            run = run_ref[((t_at * Z + z_at) * YH + y) * YL + yl]
            later = (k_runs < run) if kind else (k_runs > run)
            hidden = jnp.where(later & (lane < OWN), mask_floor, 0.0)
            if part == 0:
                hidden = own_s[yl] * jnp.where(y == yh_at, 1.0, 0.0) + hidden
            blocks.append(jnp.broadcast_to(hidden, (LANES, HD)).astype(bf))
        return jnp.concatenate(blocks, axis=0)

    def produce(kind, y, s_ref):
        q_tile = tile(kind, y)
        q_wide = jnp.concatenate([q_tile, bias(kind, y)], axis=1)
        pieces = [(slice(kind * PART, (kind + 1) * PART), q_wide)]
        if kind:
            pieces.append((slice(0, PART), q_tile))
        top = None
        for rows, q in pieces:
            s = lax.dot_general(
                k_s[rows, : q.shape[1]], q, (((1,), (1,)), ((), ())), preferred_element_type=f32
            )
            s_ref[rows, :] = s
            best = jnp.max(s.reshape(PART // 8, 8, 2 * LANES), axis=0)
            top = best if top is None else jnp.maximum(top, best)
        return jnp.max(top, axis=0, keepdims=True)

    def consume(kind, y, s_ref, top):
        total = jnp.zeros((8, 2 * LANES), f32)
        n = (kind + 1) * PART
        for at in range(0, n, PART):
            rows = slice(at, at + PART)
            w = jnp.exp2((s_ref[rows, :] - top) * LOG2_SCALE)
            total = total + jnp.sum(w.reshape(PART // 8, 8, 2 * LANES), axis=0)
            w_s[kind, rows, :] = w.astype(bf)
        total = jnp.sum(total, axis=0, keepdims=True)
        o = lax.dot_general(
            vt_s[:, :n], w_s[kind, :n, :], (((1,), (0,)), ((), ())), preferred_element_type=f32
        )
        if part == 0:
            acc_ref[y, kind] = o
            st_ref[y, kind, 0:1, :] = top
            st_ref[y, kind, 1:2, :] = total
            return None
        before = st_ref[y, kind, 0:1, :]
        best = jnp.maximum(top, before)
        keep = jnp.exp2((before - best) * LOG2_SCALE)
        add = jnp.exp2((top - best) * LOG2_SCALE)
        total = total * add + st_ref[y, kind, 1:2, :] * keep
        scale = 1.0 / total
        o = (o * (add * scale) + acc_ref[y, kind] * (keep * scale)).astype(bf)
        for t in range(YL):
            cols = slice(t * LANES, (t + 1) * LANES)
            o_ref[y, t, kind * HD : (kind + 1) * HD, :] = o[:, cols]
        lse = best * LOG2_SCALE + jnp.log2(total)
        hi = lse.astype(bf).astype(f32)
        mid = (lse - hi).astype(bf).astype(f32)
        return [hi, mid, lse - hi - mid]

    def step(y, top_e):
        top_l = produce(1, y, sl_s)
        early = consume(0, y, se_s, top_e)
        top_e = produce(0, jnp.minimum(y + 1, YH - 1), se_s)
        late = consume(1, y, sl_s, top_l)
        if part == 1:
            pad = jnp.zeros((2, 2 * LANES), f32)
            stats = jnp.concatenate(early + late + [pad], axis=0).astype(bf)
            for t in range(YL):
                o_ref[y, t, 2 * HD :, :] = stats[:, t * LANES : (t + 1) * LANES]
        return top_e

    lax.fori_loop(0, YH, step, produce(0, 0, se_s))


def combine_kernel(r_ref, o_ref):
    f32 = jnp.float32
    for half in range(2):
        heads = []
        for t in range(YL):
            lse = []
            for y in range(YH):
                st = r_ref[y, t, 2 * HD :, :].astype(f32)
                at = 3 * half
                lse.append(st[at : at + 1] + st[at + 1 : at + 2] + st[at + 2 : at + 3])
            top = lse[0]
            for v in lse[1:]:
                top = jnp.maximum(top, v)
            ws = [jnp.exp2(v - top) for v in lse]
            total = ws[0]
            for v in ws[1:]:
                total = total + v
            acc = jnp.zeros((HD, LANES), f32)
            for y in range(YH):
                acc = acc + r_ref[y, t, half * HD : (half + 1) * HD, :].astype(f32) * ws[y]
            heads.append((acc * (1.0 / total)).T)
        for p in range(2):
            block = jnp.stack(
                [
                    heads[t][p * Q_ROWS + j * PIECE : p * Q_ROWS + (j + 1) * PIECE]
                    for t in range(YL)
                    for j in range(GROUP)
                ],
                axis=0,
            )
            at = half * HALF + p * PIECE
            o_ref[at : at + PIECE] = jnp.swapaxes(block, 0, 1).astype(jnp.bfloat16)


def in_hbm(value):
    return pltpu.with_memory_space_constraint(value, pltpu.HBM)


def per_device(queries, keys, values, run_index):
    bf, f32 = jnp.bfloat16, jnp.float32
    vmem = pl.BlockSpec(memory_space=pltpu.VMEM)
    hbm = pl.BlockSpec(memory_space=pltpu.HBM)
    packed = pl.pallas_call(
        pack_kernel,
        out_shape=jax.ShapeDtypeStruct((X * YL, (GROUP + 2) * PIECE, HD), bf),
        in_specs=[hbm] * 5,
        out_specs=vmem,
        scratch_shapes=[pltpu.SMEM((SLOTS,), jnp.int32), pltpu.VMEM((1, HD), jnp.float32)]
        + [pltpu.VMEM(a.shape[1:], bf) for a in (queries, keys, values)]
        + [pltpu.SemaphoreType.DMA((5,))],
        compiler_params=pltpu.CompilerParams(vmem_limit_bytes=8 << 20),
        name="pack",
    )(*map(in_hbm, (run_index, jnp.asarray(inverse_freqs()), queries, keys, values)))
    mine = lax.all_to_all(packed, ("heads", "yl"), split_axis=0, concat_axis=0, tiled=True)
    q_own, kv_own = pl.pallas_call(
        spread_kernel,
        out_shape=(
            jax.ShapeDtypeStruct((YH, X * YL * Q_ROWS, HD), bf),
            jax.ShapeDtypeStruct((X * YL * 2 * PIECE, HD), bf),
        ),
        in_specs=[vmem],
        out_specs=(vmem, vmem),
        compiler_params=pltpu.CompilerParams(vmem_limit_bytes=8 << 20),
        name="spread",
    )(mine)
    q_all = lax.all_to_all(q_own, "yh", split_axis=0, concat_axis=0, tiled=True)
    near = lax.all_gather(kv_own, "z", axis=0, tiled=False)
    far = lax.ppermute(near, "team", [(0, 1), (1, 0)])
    kv_shape = (Z, X, YL, 2, PIECE, HD)
    q_all = q_all.reshape(YH, X, YL, Q_ROWS, HD)
    f32 = jnp.float32

    def attend(part, kv, *state):
        if part == 0:
            out = (
                jax.ShapeDtypeStruct((YH, 2, HD, 2 * LANES), f32),
                jax.ShapeDtypeStruct((YH, 2, 8, 2 * LANES), f32),
            )
        else:
            out = jax.ShapeDtypeStruct((YH, YL, MSG, LANES), bf)
        scratch = [
            pltpu.VMEM((2 * PART, 2 * HD), bf),
            pltpu.VMEM((HD, 2 * PART), bf),
            pltpu.VMEM((PART, 2 * LANES), f32),
            pltpu.VMEM((2 * PART, 2 * LANES), f32),
            pltpu.VMEM((2, 2 * PART, 2 * LANES), bf),
        ]
        return pl.pallas_call(
            functools.partial(attend_kernel, part),
            out_shape=out,
            in_specs=[hbm, vmem, vmem] + [vmem] * len(state),
            out_specs=(vmem, vmem) if part == 0 else vmem,
            scratch_shapes=scratch
            + [pltpu.VMEM((YL, LANES, HD), f32)] * (part == 0)
            + [pltpu.SMEM((SLOTS,), jnp.int32), pltpu.SemaphoreType.DMA],
            compiler_params=pltpu.CompilerParams(vmem_limit_bytes=20 << 20),
            name=("attend_near", "attend_far")[part],
        )(in_hbm(run_index), q_all, kv.reshape(kv_shape), *state)

    partial = attend(1, far, *attend(0, near))
    parts = lax.all_to_all(
        partial.reshape(Y, MSG, LANES), ("yh", "yl"), split_axis=0, concat_axis=0, tiled=True
    )
    return pl.pallas_call(
        combine_kernel,
        out_shape=jax.ShapeDtypeStruct((2 * HALF, YL * GROUP, HD), bf),
        in_specs=[vmem],
        out_specs=vmem,
        compiler_params=pltpu.CompilerParams(vmem_limit_bytes=8 << 20),
        name="combine",
    )(parts.reshape(YH, YL, MSG, LANES))


def solution(mesh):
    axes = ("heads", "team", "z", "yh", "yl")
    split = Mesh(mesh.devices.reshape(X, T, Z, YH, YL), axes)
    spec = P("heads", axes[1:], None, None)
    return jax.shard_map(
        per_device,
        mesh=split,
        in_specs=(spec, spec, spec, P()),
        out_specs=P(axes[1:], "heads", None),
        check_vma=False,
    )
```

```python
import functools
import math

import jax
import jax.numpy as jnp
import numpy as np
from jax import lax
from jax.experimental import pallas as pl
from jax.experimental.pallas import tpu as pltpu
from jax.sharding import Mesh, PartitionSpec as P

mask_floor = -1e30
rope_theta = 500000.0
rope_factor = 8.0
low_factor = 1.0
high_factor = 4.0
initial_context = 8192.0

X, T, Z, YH, YL = 4, 2, 12, 4, 2
Y = YH * YL
PIECE = 16
HALF = 32
GROUP = 4
HD = 128
SLOTS = T * Z * Y
Q_ROWS = GROUP * PIECE
PART = Z * YL * 2 * PIECE
LANES = 2 * Q_ROWS
OWN = Z * YL
MSG = 2 * HD + 8
LOG2_SCALE = HD ** -0.5 * math.log2(math.e)


def inverse_freqs():
    counter = np.arange(HD // 2, dtype=np.float64)
    base_freq = 1.0 / rope_theta ** (2.0 * counter / HD)
    wavelength = 2.0 * np.pi / base_freq
    smooth = (initial_context / wavelength - low_factor) / (high_factor - low_factor)
    blended = (1.0 - smooth) * base_freq / rope_factor + smooth * base_freq
    middle = np.where(wavelength > initial_context / low_factor, base_freq / rope_factor, blended)
    freqs = np.where(wavelength < initial_context / high_factor, base_freq, middle)
    return np.concatenate([freqs, freqs])[None, :].astype(np.float32)


def pack_kernel(
    run_hbm, freq_hbm, q_hbm, k_hbm, v_hbm, o_ref, run_ref, freq_ref, q_ref, k_ref, v_ref, sems
):
    f32 = jnp.float32
    pairs = (
        (run_hbm, run_ref),
        (freq_hbm, freq_ref),
        (q_hbm.at[0], q_ref),
        (k_hbm.at[0], k_ref),
        (v_hbm.at[0], v_ref),
    )
    moves = [pltpu.make_async_copy(a, b, sems.at[i]) for i, (a, b) in enumerate(pairs)]
    for move in moves:
        move.start()
    for move in moves[:2]:
        move.wait()
    x_at, t_at = lax.axis_index("heads"), lax.axis_index("team")
    z_at, y_at = lax.axis_index("z"), lax.axis_index("yh") * YL + lax.axis_index("yl")
    run = run_ref[(t_at * Z + z_at) * Y + y_at]
    base = jnp.where(x_at < 2, run * HALF, (2 * SLOTS - 1 - run) * HALF - HALF) + x_at * PIECE
    pos = lax.broadcasted_iota(jnp.int32, (PIECE, HD), 0) + base
    angles = pos.astype(f32) * freq_ref[...]
    cosine = jnp.cos(angles)[:, None, :]
    flip = jnp.where(lax.broadcasted_iota(jnp.int32, (PIECE, HD), 1) < HD // 2, -1.0, 1.0)
    sine = (jnp.sin(angles) * flip)[:, None, :]

    def turned(ref):
        x = ref[...].astype(f32)
        y = x * cosine + jnp.roll(x, HD // 2, axis=-1) * sine
        return jnp.swapaxes(y, 0, 1).astype(jnp.bfloat16)

    for move in moves[2:]:
        move.wait()
    n_g = k_ref.shape[1]
    o_ref[:, :Q_ROWS, :] = turned(q_ref).reshape(n_g, GROUP * PIECE, HD)
    o_ref[:, Q_ROWS : Q_ROWS + PIECE, :] = turned(k_ref)
    v = jnp.swapaxes(v_ref[...].astype(f32), 0, 1).astype(jnp.bfloat16)
    o_ref[:, Q_ROWS + PIECE :, :] = v


def spread_kernel(mine_ref, q_hbm, kv_ref, sems):
    moves = [
        pltpu.make_async_copy(mine_ref.at[:, :Q_ROWS, :], q_hbm.at[i], sems.at[i])
        for i in range(YH)
    ]
    for move in moves:
        move.start()
    kv_ref[...] = mine_ref[:, Q_ROWS:, :].reshape(X * YL * 2 * PIECE, HD)
    for move in moves:
        move.wait()


def attend_kernel(part, run_hbm, q_ref, kv_ref, *refs):
    bf, f32 = jnp.bfloat16, jnp.float32
    *refs, run_ref, sem = refs
    fetch = pltpu.make_async_copy(run_hbm, run_ref, sem)
    fetch.start()
    if part == 0:
        acc_ref, st_ref, k_s, vt_s, se_s, sl_s, w_s, own_s = refs
    else:
        acc_ref, st_ref, o_ref, k_s, vt_s, se_s, sl_s, w_s = refs
    t_at, z_at, yh_at = lax.axis_index("team"), lax.axis_index("z"), lax.axis_index("yh")
    row = lax.broadcasted_iota(jnp.int32, (PIECE, HD), 0)
    col = lax.broadcasted_iota(jnp.int32, (PIECE, HD), 1)
    lane = lax.broadcasted_iota(jnp.int32, (1, HD), 1)
    k_runs = jnp.zeros((1, HD), jnp.int32)
    team = t_at if part == 0 else 1 - t_at
    for half in range(2):
        picked = kv_ref[:, 2 * half : 2 * half + 2]
        rows = slice(half * PART, (half + 1) * PART)
        k_s[rows, :HD] = picked[:, :, :, 0].reshape(PART, HD)
        vt_s[:, rows] = picked[:, :, :, 1].reshape(PART, HD).T
    fetch.wait()
    for z in range(Z):
        for yl in range(YL):
            slot = z * YL + yl
            run = run_ref[((team * Z + z) * YH + yh_at) * YL + yl]
            k_runs = jnp.where(lane == slot, run, k_runs)
            for x in range(2):
                hot = col == slot
                if part == 0:
                    first = jnp.where(z_at == z, OWN + yl * HALF + x * PIECE, HD)
                    hot = hot | (col == row + first)
                hot = jnp.where(hot, 1.0, 0.0).astype(bf)
                for half in range(2):
                    at = half * PART + ((z * 2 + x) * YL + yl) * PIECE
                    k_s[at : at + PIECE, HD:] = hot
    if part == 0:
        q_row = lax.broadcasted_iota(jnp.int32, (LANES, HD), 0)
        q_local = (q_row // Q_ROWS) * PIECE + q_row % PIECE
        k_local = lax.broadcasted_iota(jnp.int32, (LANES, HD), 1) - OWN
        for yl in range(YL):
            after = k_local - yl * HALF
            hidden = (after > q_local) & (after < HALF)
            own_s[yl] = jnp.where(hidden, mask_floor, 0.0)

    def tile(kind, y):
        return jnp.concatenate(
            [q_ref[y, 2 * kind + x, t] for t in range(YL) for x in range(2)], axis=0
        )

    def bias(kind, y):
        blocks = []
        for yl in range(YL):
            run = run_ref[((t_at * Z + z_at) * YH + y) * YL + yl]
            later = (k_runs < run) if kind else (k_runs > run)
            hidden = jnp.where(later & (lane < OWN), mask_floor, 0.0)
            if part == 0:
                hidden = own_s[yl] * jnp.where(y == yh_at, 1.0, 0.0) + hidden
            blocks.append(jnp.broadcast_to(hidden, (LANES, HD)).astype(bf))
        return jnp.concatenate(blocks, axis=0)

    def produce(kind, y, s_ref):
        q_tile = tile(kind, y)
        q_wide = jnp.concatenate([q_tile, bias(kind, y)], axis=1)
        pieces = [(slice(kind * PART, (kind + 1) * PART), q_wide)]
        if kind:
            pieces.append((slice(0, PART), q_tile))
        top = None
        for rows, q in pieces:
            s = lax.dot_general(
                k_s[rows, : q.shape[1]], q, (((1,), (1,)), ((), ())), preferred_element_type=f32
            )
            s_ref[rows, :] = s
            best = jnp.max(s.reshape(PART // 8, 8, 2 * LANES), axis=0)
            top = best if top is None else jnp.maximum(top, best)
        return jnp.max(top, axis=0, keepdims=True)

    def consume(kind, y, s_ref, top):
        total = jnp.zeros((8, 2 * LANES), f32)
        n = (kind + 1) * PART
        for at in range(0, n, PART):
            rows = slice(at, at + PART)
            w = jnp.exp2((s_ref[rows, :] - top) * LOG2_SCALE)
            total = total + jnp.sum(w.reshape(PART // 8, 8, 2 * LANES), axis=0)
            w_s[kind, rows, :] = w.astype(bf)
        total = jnp.sum(total, axis=0, keepdims=True)
        o = lax.dot_general(
            vt_s[:, :n], w_s[kind, :n, :], (((1,), (0,)), ((), ())), preferred_element_type=f32
        )
        if part == 0:
            acc_ref[y, kind] = o
            st_ref[y, kind, 0:1, :] = top
            st_ref[y, kind, 1:2, :] = total
            return None
        before = st_ref[y, kind, 0:1, :]
        best = jnp.maximum(top, before)
        keep = jnp.exp2((before - best) * LOG2_SCALE)
        add = jnp.exp2((top - best) * LOG2_SCALE)
        total = total * add + st_ref[y, kind, 1:2, :] * keep
        scale = 1.0 / total
        o = (o * (add * scale) + acc_ref[y, kind] * (keep * scale)).astype(bf)
        for t in range(YL):
            cols = slice(t * LANES, (t + 1) * LANES)
            o_ref[y, t, kind * HD : (kind + 1) * HD, :] = o[:, cols]
        lse = best * LOG2_SCALE + jnp.log2(total)
        hi = lse.astype(bf).astype(f32)
        mid = (lse - hi).astype(bf).astype(f32)
        return [hi, mid, lse - hi - mid]

    def step(y, top_e):
        top_l = produce(1, y, sl_s)
        early = consume(0, y, se_s, top_e)
        top_e = produce(0, jnp.minimum(y + 1, YH - 1), se_s)
        late = consume(1, y, sl_s, top_l)
        if part == 1:
            pad = jnp.zeros((2, 2 * LANES), f32)
            stats = jnp.concatenate(early + late + [pad], axis=0).astype(bf)
            for t in range(YL):
                o_ref[y, t, 2 * HD :, :] = stats[:, t * LANES : (t + 1) * LANES]
        return top_e

    lax.fori_loop(0, YH, step, produce(0, 0, se_s))


def combine_kernel(r_ref, o_ref):
    f32 = jnp.float32
    for half in range(2):
        heads = []
        for t in range(YL):
            lse = []
            for y in range(YH):
                st = r_ref[y, t, 2 * HD :, :].astype(f32)
                at = 3 * half
                lse.append(st[at : at + 1] + st[at + 1 : at + 2] + st[at + 2 : at + 3])
            top = lse[0]
            for v in lse[1:]:
                top = jnp.maximum(top, v)
            ws = [jnp.exp2(v - top) for v in lse]
            total = ws[0]
            for v in ws[1:]:
                total = total + v
            acc = jnp.zeros((HD, LANES), f32)
            for y in range(YH):
                acc = acc + r_ref[y, t, half * HD : (half + 1) * HD, :].astype(f32) * ws[y]
            heads.append((acc * (1.0 / total)).T)
        for p in range(2):
            block = jnp.stack(
                [
                    heads[t][p * Q_ROWS + j * PIECE : p * Q_ROWS + (j + 1) * PIECE]
                    for t in range(YL)
                    for j in range(GROUP)
                ],
                axis=0,
            )
            at = half * HALF + p * PIECE
            o_ref[at : at + PIECE] = jnp.swapaxes(block, 0, 1).astype(jnp.bfloat16)


def in_hbm(value):
    return pltpu.with_memory_space_constraint(value, pltpu.HBM)


def per_device(queries, keys, values, run_index):
    bf, f32 = jnp.bfloat16, jnp.float32
    vmem = pl.BlockSpec(memory_space=pltpu.VMEM)
    hbm = pl.BlockSpec(memory_space=pltpu.HBM)
    packed = pl.pallas_call(
        pack_kernel,
        out_shape=jax.ShapeDtypeStruct((X * YL, (GROUP + 2) * PIECE, HD), bf),
        in_specs=[hbm] * 5,
        out_specs=vmem,
        scratch_shapes=[pltpu.SMEM((SLOTS,), jnp.int32), pltpu.VMEM((1, HD), jnp.float32)]
        + [pltpu.VMEM(a.shape[1:], bf) for a in (queries, keys, values)]
        + [pltpu.SemaphoreType.DMA((5,))],
        compiler_params=pltpu.CompilerParams(vmem_limit_bytes=8 << 20),
        name="pack",
    )(*map(in_hbm, (run_index, jnp.asarray(inverse_freqs()), queries, keys, values)))
    mine = lax.all_to_all(packed, ("heads", "yl"), split_axis=0, concat_axis=0, tiled=True)
    q_own, kv_own = pl.pallas_call(
        spread_kernel,
        out_shape=(
            jax.ShapeDtypeStruct((YH, X * YL, Q_ROWS, HD), bf),
            jax.ShapeDtypeStruct((X * YL * 2 * PIECE, HD), bf),
        ),
        in_specs=[vmem],
        out_specs=(hbm, vmem),
        scratch_shapes=[pltpu.SemaphoreType.DMA((YH,))],
        compiler_params=pltpu.CompilerParams(vmem_limit_bytes=8 << 20),
        name="spread",
    )(mine)
    q_all = lax.all_to_all(q_own, "yh", split_axis=0, concat_axis=0, tiled=True)
    near = lax.all_gather(kv_own, "z", axis=0, tiled=False)
    far = lax.ppermute(near, "team", [(0, 1), (1, 0)])
    kv_shape = (Z, X, YL, 2, PIECE, HD)
    q_all = q_all.reshape(YH, X, YL, Q_ROWS, HD)
    f32 = jnp.float32

    def attend(part, kv, *state):
        if part == 0:
            out = (
                jax.ShapeDtypeStruct((YH, 2, HD, 2 * LANES), f32),
                jax.ShapeDtypeStruct((YH, 2, 8, 2 * LANES), f32),
            )
        else:
            out = jax.ShapeDtypeStruct((YH, YL, MSG, LANES), bf)
        scratch = [
            pltpu.VMEM((2 * PART, 2 * HD), bf),
            pltpu.VMEM((HD, 2 * PART), bf),
            pltpu.VMEM((PART, 2 * LANES), f32),
            pltpu.VMEM((2 * PART, 2 * LANES), f32),
            pltpu.VMEM((2, 2 * PART, 2 * LANES), bf),
        ]
        return pl.pallas_call(
            functools.partial(attend_kernel, part),
            out_shape=out,
            in_specs=[hbm, vmem, vmem] + [vmem] * len(state),
            out_specs=(vmem, vmem) if part == 0 else vmem,
            scratch_shapes=scratch
            + [pltpu.VMEM((YL, LANES, HD), f32)] * (part == 0)
            + [pltpu.SMEM((SLOTS,), jnp.int32), pltpu.SemaphoreType.DMA],
            compiler_params=pltpu.CompilerParams(vmem_limit_bytes=20 << 20),
            name=("attend_near", "attend_far")[part],
        )(in_hbm(run_index), q_all, kv.reshape(kv_shape), *state)

    partial = attend(1, far, *attend(0, near))
    parts = lax.all_to_all(
        partial.reshape(Y, MSG, LANES), ("yh", "yl"), split_axis=0, concat_axis=0, tiled=True
    )
    return pl.pallas_call(
        combine_kernel,
        out_shape=jax.ShapeDtypeStruct((2 * HALF, YL * GROUP, HD), bf),
        in_specs=[vmem],
        out_specs=vmem,
        compiler_params=pltpu.CompilerParams(vmem_limit_bytes=8 << 20),
        name="combine",
    )(parts.reshape(YH, YL, MSG, LANES))


def solution(mesh):
    axes = ("heads", "team", "z", "yh", "yl")
    split = Mesh(mesh.devices.reshape(X, T, Z, YH, YL), axes)
    spec = P("heads", axes[1:], None, None)
    return jax.shard_map(
        per_device,
        mesh=split,
        in_specs=(spec, spec, spec, P()),
        out_specs=P(axes[1:], "heads", None),
        check_vma=False,
    )
```
